32 devices in a mesh: ax: 8 (over z, y), az: 4 (over x, core).
Axes of the slice: x: 2, y: 2, z: 4, core: 2. Of those that a mesh axis runs over, the one named last changes fastest.
Arguments:
- density: float32 [32, 256, 256], P('ax', 'az'), may hold values from 0.5 to 2
- velocity: float32 [3, 32, 256, 256], P(None, 'ax', 'az'), may hold values from -12 to 12
Outputs:
- stress_flux: float32 [3, 32, 256, 256], P(None, 'ax', 'az')
- coefficient: float32 [32, 256], P('ax')
The draws below stay inside these ranges and needn't reach their ends.
All inputs are finite; a program needn't handle non-finite values.
Results may differ from the reference program's by a relative error of at most 0.00002.
Values sent between devices are 32-bit elements; how exact they have to be, the bound alone decides.
A program may use at most 64 MiB of HBM per device.

```python
import math
import jax
import jax.numpy as jnp
from jax import lax

NR = 256
NX = 32
NT = 256


def draw_velocity(key, part):
    sector_at = jnp.arange(NT, dtype=jnp.float32) / NT
    amplitude = (0.5 + sector_at)[None, None, :, None]
    random_part = jnp.clip(jax.random.normal(key, (3, NX, NT, NR), jnp.float32), -6.0, 6.0)
    return random_part * amplitude


def levels(rng, shape, cuts, least, top_value):
    factor_of = 1.0
    for axis_at, blocks in cuts:
        draws = jax.random.uniform(jax.random.fold_in(jax.random.fold_in(rng, 6), axis_at), (blocks,), jnp.float32, least / len(cuts), top_value / len(cuts))
        factor_of = factor_of * jnp.repeat(jnp.exp(draws), shape[axis_at] // blocks).reshape((-1,) + (1,) * (len(shape) - 1 - axis_at))
    return factor_of


def setup_inputs(seed: int = 0) -> dict:
    splits = jax.random.split(jax.random.key(seed), 3)
    density = jnp.clip(0.5 + 1.5 * jax.random.uniform(splits[0], (NX, NT, NR), jnp.float32) ** levels(splits[0], (NX, NT, NR), ((0, 8), (1, 4)), -0.2, 0.2), 0.5, 2.0)
    velocity = draw_velocity(jax.random.fold_in(splits[2], 71), 0)
    return {"density": density, "velocity": velocity}


STEP_AXIAL = 0.5
STEP_RADIAL = 0.25
INNER_RADIUS = 10.0
FILTER_RATIO = 2.0
TINY = 1e-06
COMPONENT_PAIRS = ((0, 0), (1, 1), (2, 2), (0, 1), (0, 2), (1, 2))

def trim_cells(values, dim_at, amount):
    extent = values.shape[dim_at]
    return lax.slice_in_dim(values, amount, extent - amount, axis=dim_at)

def interior(values, amount):
    values = trim_cells(values, values.ndim - 3, amount)
    return trim_cells(values, values.ndim - 2, amount)

def pad_radial(values):
    return jnp.concatenate([values[..., :1], values, values[..., -1:]], axis=values.ndim - 1)

def smooth_axis(values, dim_at):
    extent = values.shape[dim_at]
    return 0.25 * lax.slice_in_dim(values, 0, extent - 2, axis=dim_at) + 0.5 * lax.slice_in_dim(values, 1, extent - 1, axis=dim_at) + 0.25 * lax.slice_in_dim(values, 2, extent, axis=dim_at)

def slope_axis(values, dim_at):
    extent = values.shape[dim_at]
    return 0.5 * (lax.slice_in_dim(values, 2, extent, axis=dim_at) - lax.slice_in_dim(values, 0, extent - 2, axis=dim_at))

def test_filter(values):
    smooth = smooth_axis(values, values.ndim - 3)
    smooth = smooth_axis(smooth, values.ndim - 2)
    return smooth_axis(pad_radial(smooth), values.ndim - 1)

def geometry(radial_cells, azimuth_cells):
    radius = INNER_RADIUS + (jnp.arange(radial_cells, dtype=jnp.float32) + 0.5) * STEP_RADIAL
    angle_step = 2.0 * math.pi / azimuth_cells
    width_sq = (STEP_AXIAL * STEP_RADIAL * angle_step * radius) ** (2.0 / 3.0)
    return (radius, angle_step, width_sq)

def strain(velocity, radius, angle_step):
    d_ax = trim_cells(slope_axis(velocity, 1), 2, 1) / STEP_AXIAL
    d_az = trim_cells(slope_axis(velocity, 2), 1, 1) / (radius * angle_step)
    d_rad = interior(slope_axis(pad_radial(velocity), 3), 1) / STEP_RADIAL
    centre = interior(velocity, 1)
    s_xx = d_ax[0]
    s_rr = d_rad[1]
    s_tt = d_az[2] + centre[1] / radius
    s_xr = 0.5 * (d_rad[0] + d_ax[1])
    s_xt = 0.5 * (d_az[0] + d_ax[2])
    s_rt = 0.5 * (d_az[1] + d_rad[2] - centre[2] / radius)
    strength = jnp.sqrt(2.0 * (s_xx * s_xx + s_rr * s_rr + s_tt * s_tt + 2.0 * (s_xr * s_xr + s_xt * s_xt + s_rt * s_rt)))
    third = (s_xx + s_rr + s_tt) / 3.0
    deviator = jnp.stack([s_xx - third, s_rr - third, s_tt - third, s_xr, s_xt, s_rt])
    return (deviator, strength)

def model_of(density, width_sq, strength, deviator):
    return density * width_sq * strength * deviator

def pair_products(left_v, right_v):
    return jnp.stack([left_v[first_c] * right_v[second_c] for first_c, second_c in COMPONENT_PAIRS])

def contract(left_t, right_t):
    return left_t[0] * right_t[0] + left_t[1] * right_t[1] + left_t[2] * right_t[2] + 2.0 * (left_t[3] * right_t[3] + left_t[4] * right_t[4] + left_t[5] * right_t[5])

def closure(hat_rho, hat_mom, hat_pairs, hat_model, hat_dev, hat_strength, width_sq):
    mixed_term = FILTER_RATIO * FILTER_RATIO * width_sq * hat_rho * hat_strength * hat_dev - hat_model
    resolved = jnp.stack([hat_mom[first_c] * hat_mom[second_c] / hat_rho for first_c, second_c in COMPONENT_PAIRS])
    leonard = hat_pairs - resolved
    return (contract(leonard, mixed_term), contract(mixed_term, mixed_term))

def lilly_ratio(lm_sum, mm_sum, azimuth_cells):
    return -0.5 * (lm_sum / azimuth_cells) / (mm_sum / azimuth_cells + TINY)

def divergence(stress, radius, angle_step):
    d_ax = trim_cells(slope_axis(stress, 1), 2, 1) / STEP_AXIAL
    d_az = trim_cells(slope_axis(stress, 2), 1, 1) / (radius * angle_step)
    radial_one = pad_radial(jnp.stack([stress[3], stress[1]]) * radius)
    radial_two = pad_radial(stress[5] * (radius * radius))
    d_one = interior(slope_axis(radial_one, 3), 1) / STEP_RADIAL / radius
    d_two = interior(slope_axis(radial_two, 2), 1) / STEP_RADIAL / (radius * radius)
    centre = interior(stress, 1)
    flux_x = d_ax[0] + d_one[0] + d_az[4]
    flux_r = d_ax[3] + d_one[1] + d_az[5] - centre[2] / radius
    flux_t = d_ax[4] + d_two + d_az[2]
    return jnp.stack([flux_x, flux_r, flux_t])

def pad_cells(values, width_cells):
    leading = [(0, 0)] * (values.ndim - 3)
    values = jnp.pad(values, leading + [(width_cells, width_cells), (0, 0), (0, 0)], mode='edge')
    return jnp.pad(values, leading + [(0, 0), (width_cells, width_cells), (0, 0)], mode='wrap')

def reference(density, velocity):
    radius, angle_step, width_sq = geometry(NR, NT)
    deviator, strength = strain(pad_cells(velocity, 1), radius, angle_step)
    model_stress = model_of(density, width_sq, strength, deviator)
    momentum = density * velocity
    pair_terms = pair_products(momentum, velocity)
    hat_rho = test_filter(pad_cells(density, 1))
    hat_mom = test_filter(pad_cells(momentum, 1))
    hat_pairs = test_filter(pad_cells(pair_terms, 1))
    hat_model = test_filter(pad_cells(model_stress, 1))
    hat_dev, hat_strength = strain(pad_cells(hat_mom / hat_rho, 1), radius, angle_step)
    lm_cells, mm_cells = closure(hat_rho, hat_mom, hat_pairs, hat_model, hat_dev, hat_strength, width_sq)
    coefficient = lilly_ratio(lax.optimization_barrier(jnp.sum(lm_cells, axis=1)), lax.optimization_barrier(jnp.sum(mm_cells, axis=1)), NT)
    stress = -2.0 * coefficient[:, None, :] * model_stress
    stress_flux = divergence(pad_cells(stress, 1), radius, angle_step)
    return (stress_flux, coefficient)
```

```python
import functools
import math

import jax
import jax.numpy as jnp
import numpy as np
from jax import lax
from jax.experimental import pallas as pl
from jax.experimental.pallas import tpu as pltpu
from jax.sharding import PartitionSpec as P

STEP_AXIAL = 0.5
STEP_RADIAL = 0.25
INNER_RADIUS = 10.0
FILTER_RATIO = 2.0
TINY = 1e-06
PAIRS = ((0, 0), (1, 1), (2, 2), (0, 1), (0, 2), (1, 2))
LANES = 128
SUB = 8
EDGE = 16
MESH_ID = pl.DeviceIdType.MESH


def geometry(radial, azimuth_cells):
    radius = INNER_RADIUS + (np.arange(radial, dtype=np.float64) + 0.5) * STEP_RADIAL
    angle = 2.0 * math.pi / azimuth_cells
    width = (STEP_AXIAL * STEP_RADIAL * angle * radius) ** (2.0 / 3.0)
    rows = np.stack(
        [
            1.0 / radius,
            0.5 / (radius * angle),
            width,
            FILTER_RATIO**2 * width,
            radius,
            0.5 / STEP_RADIAL / radius,
            radius * radius,
            0.5 / STEP_RADIAL / (radius * radius),
        ]
    ).astype(np.float32)
    rows = rows.reshape(rows.shape[0], radial // LANES, 1, LANES)
    return np.ascontiguousarray(np.broadcast_to(rows, rows.shape[:2] + (SUB, LANES)))


def before(x):
    lane = lax.broadcasted_iota(jnp.int32, x.shape, x.ndim - 1)
    y = pltpu.roll(x, 1, x.ndim - 1)
    fill = jnp.concatenate([x[:1], y[:-1]], axis=0)
    return jnp.where(lane == 0, fill, y)


def after(x):
    lane = lax.broadcasted_iota(jnp.int32, x.shape, x.ndim - 1)
    y = pltpu.roll(x, LANES - 1, x.ndim - 1)
    fill = jnp.concatenate([y[1:], x[-1:]], axis=0)
    return jnp.where(lane == LANES - 1, fill, y)


def rise(x):
    return after(x) - before(x)


def strain(dx, dr, dt, ur, ut, inv_r):
    s_xx, s_rr = dx[0], dr[1]
    s_tt = dt[2] + ur * inv_r
    s_xr = 0.5 * (dr[0] + dx[1])
    s_xt = 0.5 * (dt[0] + dx[2])
    s_rt = 0.5 * (dt[1] + dr[2] - ut * inv_r)
    size = jnp.sqrt(
        2.0
        * (
            s_xx * s_xx
            + s_rr * s_rr
            + s_tt * s_tt
            + 2.0 * (s_xr * s_xr + s_xt * s_xt + s_rt * s_rt)
        )
    )
    third = (s_xx + s_rr + s_tt) * (1.0 / 3.0)
    return (s_xx - third, s_rr - third, s_tt - third, s_xr, s_xt, s_rt), size


def kernel(
    n_ax, n_az, nx, nt, nh,
    rho_ref, vel_ref, geo_ref, flux_ref, coef_ref,
    S, M, H, V, HM, PX, MX, ACC, part, rec, rec_lo, rec_hi, CS,
    own_sem, halo_send, halo_recv, corner_send, corner_recv, sum_send, sum_recv,
):
    me_ax, me_az = lax.axis_index("ax"), lax.axis_index("az")
    left, right = lax.rem(me_az + n_az - 1, n_az), lax.rem(me_az + 1, n_az)
    has_lo, has_hi = me_ax > 0, me_ax < n_ax - 1
    azimuth_cells = nt * n_az

    own = []
    for h in range(nh):
        lanes = pl.ds(h * LANES, LANES)
        cols = pl.ds(EDGE, nt)
        own.append(pltpu.make_async_copy(
            rho_ref.at[:, :, lanes], S.at[0, pl.ds(2, nx), h, cols, :], own_sem.at[2 * h]))
        own.append(pltpu.make_async_copy(
            vel_ref.at[:, :, :, lanes], S.at[pl.ds(1, 3), pl.ds(2, nx), h, cols, :], own_sem.at[2 * h + 1]))
    for c in own:
        c.start()

    barrier = pltpu.get_barrier_semaphore()

    def greet(ax, az):
        pl.semaphore_signal(barrier, inc=1, device_id=(ax, az), device_id_type=MESH_ID)

    for d in range(1, n_az):
        greet(me_ax, lax.rem(me_az + d, n_az))

    @pl.when(has_lo)
    def _():
        for d in range(n_az):
            greet(me_ax - 1, lax.rem(me_az + d, n_az))

    @pl.when(has_hi)
    def _():
        for d in range(n_az):
            greet(me_ax + 1, lax.rem(me_az + d, n_az))

    peers = n_az - 1 + jnp.where(has_lo, n_az, 0) + jnp.where(has_hi, n_az, 0)
    pl.semaphore_wait(barrier, peers)

    def halo(kind, src_rows, src_cols, dst_rows, dst_cols, target):
        copies = []
        for h in range(nh):
            lanes = pl.ds(h * LANES, LANES)
            copies.append(pltpu.make_async_remote_copy(
                src_ref=rho_ref.at[src_rows, src_cols, lanes],
                dst_ref=S.at[0, dst_rows, h, dst_cols, :],
                send_sem=halo_send.at[kind, 2 * h], recv_sem=halo_recv.at[kind, 2 * h],
                device_id=target, device_id_type=MESH_ID))
            copies.append(pltpu.make_async_remote_copy(
                src_ref=vel_ref.at[:, src_rows, src_cols, lanes],
                dst_ref=S.at[pl.ds(1, 3), dst_rows, h, dst_cols, :],
                send_sem=halo_send.at[kind, 2 * h + 1], recv_sem=halo_recv.at[kind, 2 * h + 1],
                device_id=target, device_id_type=MESH_ID))
        return copies

    every = pl.ds(0, nt)
    mid = pl.ds(EDGE, nt)
    up = [halo(0, pl.ds(nx - 1, 1), every, pl.ds(1, 1), mid, (me_ax + 1, me_az)),
          halo(1, pl.ds(nx - 2, 1), every, pl.ds(0, 1), mid, (me_ax + 1, me_az))]
    down = [halo(2, pl.ds(0, 1), every, pl.ds(nx + 2, 1), mid, (me_ax - 1, me_az)),
            halo(3, pl.ds(1, 1), every, pl.ds(nx + 3, 1), mid, (me_ax - 1, me_az))]
    around = halo(4, pl.ds(0, nx), pl.ds(nt - SUB, SUB), pl.ds(2, nx), pl.ds(EDGE - SUB, SUB), (me_ax, right))
    around += halo(5, pl.ds(0, nx), pl.ds(0, SUB), pl.ds(2, nx), pl.ds(EDGE + nt, SUB), (me_ax, left))

    for c in around:
        c.start()
    for step in range(2):
        @pl.when(has_hi)
        def _():
            for c in up[step]:
                c.start()

        @pl.when(has_lo)
        def _():
            for c in down[step]:
                c.start()

    def corner(slot, row):
        return [
            pltpu.make_async_remote_copy(
                src_ref=S.at[:, row, :, pl.ds(EDGE + nt - SUB, SUB), :],
                dst_ref=S.at[:, row, :, pl.ds(EDGE - SUB, SUB), :],
                send_sem=corner_send.at[slot, 0], recv_sem=corner_recv.at[slot, 0],
                device_id=(me_ax, right), device_id_type=MESH_ID),
            pltpu.make_async_remote_copy(
                src_ref=S.at[:, row, :, pl.ds(EDGE, SUB), :],
                dst_ref=S.at[:, row, :, pl.ds(EDGE + nt, SUB), :],
                send_sem=corner_send.at[slot, 1], recv_sem=corner_recv.at[slot, 1],
                device_id=(me_ax, left), device_id_type=MESH_ID),
        ]

    def receive(step):
        lo_corner, hi_corner = corner(step, 1 - step), corner(2 + step, nx + 2 + step)

        @pl.when(has_lo)
        def _():
            for c in up[step]:
                c.wait_recv()
            for c in lo_corner:
                c.start()

        @pl.when(has_hi)
        def _():
            for c in down[step]:
                c.wait_recv()
            for c in hi_corner:
                c.start()

        @pl.when(has_lo)
        def _():
            for c in lo_corner:
                c.wait()

        @pl.when(has_hi)
        def _():
            for c in hi_corner:
                c.wait()

    def low(r):
        return jnp.maximum(r - 1, jnp.where(has_lo, -2, 0))

    def high(r):
        return jnp.minimum(r + 1, jnp.where(has_hi, nx + 1, nx - 1))

    def sweep(first, stride, count, tiles, body):
        def step(at, carry):
            r = first + stride * (at // tiles)
            body(r, lax.rem(at, tiles))
            return carry

        lax.fori_loop(0, count * tiles, step, 0)

    wide = nt // SUB + 2

    def near(ref, lead, row, col, shift):
        return ref[lead, row, :, pl.ds(col + shift, SUB), :]

    def tile(ref, lead, row, col):
        return ref[lead, row, :, pl.ds(pl.multiple_of(col, SUB), SUB), :]

    def put(ref, lead, row, col, value):
        ref[lead, row, :, pl.ds(pl.multiple_of(col, SUB), SUB), :] = value

    def first_pass(with_pairs):
        def body(r, t):
            c = (EDGE - SUB) + t * SUB
            rows = (low(r) + 2, r + 2, high(r) + 2)
            rho = [tile(S, 0, q, c) for q in rows]
            vel = [[tile(S, 1 + a, q, c) for a in range(3)] for q in rows]
            inv_r, az_scale, width = geo_ref[0], geo_ref[1], geo_ref[2]
            dx = [vel[2][a] - vel[0][a] for a in range(3)]
            dr = [rise(vel[1][a]) * (0.5 / STEP_RADIAL) for a in range(3)]
            dt = [(near(S, 1 + a, r + 2, c, 1) - near(S, 1 + a, r + 2, c, -1)) * az_scale for a in range(3)]
            dev, size = strain(dx, dr, dt, vel[1][1], vel[1][2], inv_r)
            scale = rho[1] * width * size
            for a in range(6):
                put(M, a, r + 1, c, scale * dev[a])
            mom = [[rho[q] * vel[q][a] for a in range(3)] for q in range(3)]
            put(H, 0, r + 1, c, (rho[0] + rho[1]) + (rho[1] + rho[2]))
            for a in range(3):
                put(H, 1 + a, r + 1, c, (mom[0][a] + mom[1][a]) + (mom[1][a] + mom[2][a]))
            if with_pairs:
                for at, (a, b) in enumerate(PAIRS):
                    p = [mom[q][a] * vel[q][b] for q in range(3)]
                    put(PX, at, r, c, (p[0] + p[1]) + (p[1] + p[2]))
        return body

    def smooth(ref, lead, row, c):
        mid_value = tile(ref, lead, row, c)
        s = (near(ref, lead, row, c, -1) + near(ref, lead, row, c, 1)) + (mid_value + mid_value)
        return ((before(s) + after(s)) + (s + s)) * (1.0 / 64.0)

    def hat_pass(r, t):
        c = (EDGE - SUB) + t * SUB
        hat = [smooth(H, a, r + 1, c) for a in range(4)]
        inv = 1.0 / hat[0]
        for a in range(4):
            put(HM, a, r + 1, c, hat[a])
        for a in range(3):
            put(V, a, r + 1, c, hat[1 + a] * inv)

    def model_pass(r, t):
        c = (EDGE - SUB) + t * SUB
        for a in range(6):
            m = tile(M, a, r + 1, c)
            put(MX, a, r, c, (tile(M, a, low(r) + 1, c) + m) + (m + tile(M, a, high(r) + 1, c)))

    def closure_pass(r, t):
        c = EDGE + t * SUB
        inv_r, az_scale, width4 = geo_ref[0], geo_ref[1], geo_ref[3]
        hv = [tile(V, a, r + 1, c) for a in range(3)]
        dx = [tile(V, a, high(r) + 1, c) - tile(V, a, low(r) + 1, c) for a in range(3)]
        dr = [rise(hv[a]) * (0.5 / STEP_RADIAL) for a in range(3)]
        dt = [(near(V, a, r + 1, c, 1) - near(V, a, r + 1, c, -1)) * az_scale for a in range(3)]
        dev, size = strain(dx, dr, dt, hv[1], hv[2], inv_r)
        scale = width4 * tile(HM, 0, r + 1, c) * size
        hm = [tile(HM, 1 + a, r + 1, c) for a in range(3)]
        lm, mm = [], []
        for at, (a, b) in enumerate(PAIRS):
            mixed = scale * dev[at] - smooth(MX, at, r, c)
            leonard = smooth(PX, at, r, c) - hm[a] * hv[b]
            lm.append(leonard * mixed)
            mm.append(mixed * mixed)
        ACC[r, 0] += (lm[0] + lm[1] + lm[2]) + 2.0 * (lm[3] + lm[4] + lm[5])
        ACC[r, 1] += (mm[0] + mm[1] + mm[2]) + 2.0 * (mm[3] + mm[4] + mm[5])

    ACC[...] = jnp.zeros_like(ACC)
    for c in own:
        c.wait()
    for c in around:
        c.wait_recv()
    sweep(1, 1, nx - 2, wide, first_pass(True))
    sweep(1, 1, nx - 2, wide, hat_pass)
    receive(0)
    sweep(0, nx - 1, 2, wide, first_pass(True))
    sweep(0, nx - 1, 2, wide, hat_pass)
    sweep(1, 1, nx - 2, wide, model_pass)
    sweep(1, 1, nx - 2, nt // SUB, closure_pass)
    receive(1)
    sweep(-1, nx + 1, 2, wide, first_pass(False))
    sweep(-1, nx + 1, 2, wide, hat_pass)
    sweep(0, nx - 1, 2, wide, model_pass)
    sweep(0, nx - 1, 2, nt // SUB, closure_pass)

    for r in range(nx):
        for q in range(2):
            for h in range(nh):
                row = jnp.sum(ACC[r, q, h], axis=0, keepdims=True)
                part[r, pl.ds(q * nh + h, 1), :] = row
                rec[me_az, r, pl.ds(q * nh + h, 1), :] = row

    def share(kind, d, src, dst, ax):
        return pltpu.make_async_remote_copy(
            src_ref=src, dst_ref=dst.at[me_az],
            send_sem=sum_send.at[kind, d], recv_sem=sum_recv.at[kind, d],
            device_id=(ax, lax.rem(me_az + d, n_az)), device_id_type=MESH_ID)

    to_hi = [share(1, d, part.at[nx - 1], rec_lo, me_ax + 1) for d in range(n_az)]
    to_lo = [share(2, d, part.at[0], rec_hi, me_ax - 1) for d in range(n_az)]
    across = [share(0, d, part, rec, me_ax) for d in range(1, n_az)]

    @pl.when(has_hi)
    def _():
        for c in to_hi:
            c.start()

    @pl.when(has_lo)
    def _():
        for c in to_lo:
            c.start()

    for c in across:
        c.start()

    def ratio(sums):
        lm, mm = sums[:nh], sums[nh:]
        return -0.5 * (lm * (1.0 / azimuth_cells)) / (mm * (1.0 / azimuth_cells) + TINY)

    def total(ref):
        sums = ref[0]
        for d in range(1, n_az):
            sums = sums + ref[d]
        return sums

    def keep(row, value):
        for h in range(nh):
            CS[row, h] = jnp.broadcast_to(-2.0 * value[h:h + 1], (SUB, LANES))

    for c in across:
        c.wait_recv()
    for r in range(nx):
        value = ratio(total(rec.at[:, r]))
        keep(r + 1, value)
        for h in range(nh):
            coef_ref[pl.ds(r, 1), pl.ds(h * LANES, LANES)] = value[h:h + 1]

    def flux_pass(r, t):
        c = EDGE + t * SUB
        inv_r, az_scale = geo_ref[0], geo_ref[1]
        radius, back, radius2, back2 = geo_ref[4], geo_ref[5], geo_ref[6], geo_ref[7]
        lo, hi = low(r) + 1, high(r) + 1
        here, below, above = CS[r + 1], CS[lo], CS[hi]

        def axial(a):
            return above * tile(M, a, hi, c) - below * tile(M, a, lo, c)

        def around_of(a):
            return (near(M, a, r + 1, c, 1) - near(M, a, r + 1, c, -1)) * turn

        turn = here * az_scale
        once = here * radius
        d_xr = rise(once * tile(M, 3, r + 1, c)) * back
        d_rr = rise(once * tile(M, 1, r + 1, c)) * back
        d_rt = rise(here * radius2 * tile(M, 5, r + 1, c)) * back2
        out = (
            axial(0) + d_xr + around_of(4),
            axial(3) + d_rr + around_of(5) - here * tile(M, 2, r + 1, c) * inv_r,
            axial(4) + d_rt + around_of(2),
        )
        rows = pl.ds(pl.multiple_of(t * SUB, SUB), SUB)
        for a in range(3):
            for h in range(nh):
                flux_ref[a, r, rows, pl.ds(h * LANES, LANES)] = out[a][h]

    sweep(1, 1, nx - 2, nt // SUB, flux_pass)

    @pl.when(has_lo)
    def _():
        for c in to_hi:
            c.wait_recv()
        keep(0, ratio(total(rec_lo)))

    @pl.when(has_hi)
    def _():
        for c in to_lo:
            c.wait_recv()
        keep(nx + 1, ratio(total(rec_hi)))

    sweep(0, nx - 1, 2, nt // SUB, flux_pass)

    for c in across + around:
        c.wait_send()

    @pl.when(has_hi)
    def _():
        for c in up[0] + up[1] + to_hi:
            c.wait_send()

    @pl.when(has_lo)
    def _():
        for c in down[0] + down[1] + to_lo:
            c.wait_send()


def shards(n_ax, n_az, density, velocity):
    nx, nt, radial = density.shape
    nh = radial // LANES
    cols = nt + 2 * EDGE
    geo = jnp.asarray(geometry(radial, nt * n_az))

    def field(count, rows):
        return pltpu.VMEM((count, rows, nh, cols, LANES), jnp.float32)

    dma = pltpu.SemaphoreType.DMA
    return pl.pallas_call(
        functools.partial(kernel, n_ax, n_az, nx, nt, nh),
        out_shape=(
            jax.ShapeDtypeStruct(velocity.shape, jnp.float32),
            jax.ShapeDtypeStruct((nx, radial), jnp.float32),
        ),
        in_specs=[
            pl.BlockSpec(memory_space=pl.ANY),
            pl.BlockSpec(memory_space=pl.ANY),
            pl.BlockSpec(memory_space=pltpu.VMEM),
        ],
        out_specs=(
            pl.BlockSpec(memory_space=pltpu.VMEM),
            pl.BlockSpec(memory_space=pltpu.VMEM),
        ),
        scratch_shapes=[
            field(4, nx + 4),
            field(6, nx + 2),
            field(4, nx + 2),
            field(3, nx + 2),
            field(4, nx + 2),
            field(6, nx),
            field(6, nx),
            pltpu.VMEM((nx, 2, nh, SUB, LANES), jnp.float32),
            pltpu.VMEM((nx, 2 * nh, LANES), jnp.float32),
            pltpu.VMEM((n_az, nx, 2 * nh, LANES), jnp.float32),
            pltpu.VMEM((n_az, 2 * nh, LANES), jnp.float32),
            pltpu.VMEM((n_az, 2 * nh, LANES), jnp.float32),
            pltpu.VMEM((nx + 2, nh, SUB, LANES), jnp.float32),
            dma((2 * nh,)),
            dma((6, 2 * nh)),
            dma((6, 2 * nh)),
            dma((4, 2)),
            dma((4, 2)),
            dma((3, n_az)),
            dma((3, n_az)),
        ],
        compiler_params=pltpu.CompilerParams(collective_id=0, has_side_effects=True),
        name="closure",
    )(density, velocity, geo)


def solution(mesh):
    in_specs = (P("ax", "az", None), P(None, "ax", "az", None))
    out_specs = (P(None, "ax", "az", None), P("ax", None))
    body = functools.partial(shards, mesh.shape["ax"], mesh.shape["az"])
    return jax.shard_map(body, mesh=mesh, in_specs=in_specs, out_specs=out_specs, check_vma=False)
```

```python
import functools
import math

import jax
import jax.numpy as jnp
import numpy as np
from jax import lax
from jax.experimental import pallas as pl
from jax.experimental.pallas import tpu as pltpu
from jax.sharding import PartitionSpec as P

STEP_AXIAL = 0.5
STEP_RADIAL = 0.25
INNER_RADIUS = 10.0
FILTER_RATIO = 2.0
TINY = 1e-06
PAIRS = ((0, 0), (1, 1), (2, 2), (0, 1), (0, 2), (1, 2))
LANES = 128
SUB = 8
BLOCKS = {"first": 5, "hat": 10, "model": 10, "closure": 4, "flux": 4}
EDGE = 16
MESH_ID = pl.DeviceIdType.MESH


def geometry(radial, azimuth_cells):
    radius = INNER_RADIUS + (np.arange(radial, dtype=np.float64) + 0.5) * STEP_RADIAL
    angle = 2.0 * math.pi / azimuth_cells
    width = (STEP_AXIAL * STEP_RADIAL * angle * radius) ** (2.0 / 3.0)
    rows = np.stack(
        [
            1.0 / radius,
            0.5 / (radius * angle),
            width,
            FILTER_RATIO**2 * width,
            radius,
            0.5 / STEP_RADIAL / radius,
            radius * radius,
            0.5 / STEP_RADIAL / (radius * radius),
        ]
    ).astype(np.float32)
    rows = rows.reshape(rows.shape[0], radial // LANES, 1, LANES)
    return np.ascontiguousarray(np.broadcast_to(rows, rows.shape[:2] + (SUB, LANES)))


def before(x):
    lane = lax.broadcasted_iota(jnp.int32, x.shape, x.ndim - 1)
    y = pltpu.roll(x, 1, x.ndim - 1)
    fill = jnp.concatenate([x[:1], y[:-1]], axis=0)
    return jnp.where(lane == 0, fill, y)


def after(x):
    lane = lax.broadcasted_iota(jnp.int32, x.shape, x.ndim - 1)
    y = pltpu.roll(x, LANES - 1, x.ndim - 1)
    fill = jnp.concatenate([y[1:], x[-1:]], axis=0)
    return jnp.where(lane == LANES - 1, fill, y)


def rise(x):
    return after(x) - before(x)


def strain(dx, dr, dt, ur, ut, inv_r):
    s_xx, s_rr = dx[0], dr[1]
    s_tt = dt[2] + ur * inv_r
    s_xr = 0.5 * (dr[0] + dx[1])
    s_xt = 0.5 * (dt[0] + dx[2])
    s_rt = 0.5 * (dt[1] + dr[2] - ut * inv_r)
    size = jnp.sqrt(
        2.0
        * (
            s_xx * s_xx
            + s_rr * s_rr
            + s_tt * s_tt
            + 2.0 * (s_xr * s_xr + s_xt * s_xt + s_rt * s_rt)
        )
    )
    third = (s_xx + s_rr + s_tt) * (1.0 / 3.0)
    return (s_xx - third, s_rr - third, s_tt - third, s_xr, s_xt, s_rt), size


def kernel(
    n_ax, n_az, nx, nt, nh,
    rho_ref, vel_ref, geo_ref, flux_ref, coef_ref,
    S, M, H, V, HM, PX, MX, ACC, part, rec, rec_lo, rec_hi, CS,
    own_sem, halo_send, halo_recv, corner_send, corner_recv, sum_send, sum_recv,
):
    me_ax, me_az = lax.axis_index("ax"), lax.axis_index("az")
    left, right = lax.rem(me_az + n_az - 1, n_az), lax.rem(me_az + 1, n_az)
    has_lo, has_hi = me_ax > 0, me_ax < n_ax - 1
    azimuth_cells = nt * n_az

    own = []
    for h in range(nh):
        lanes = pl.ds(h * LANES, LANES)
        cols = pl.ds(EDGE, nt)
        own.append(pltpu.make_async_copy(
            rho_ref.at[:, :, lanes], S.at[0, pl.ds(2, nx), h, cols, :], own_sem.at[2 * h]))
        own.append(pltpu.make_async_copy(
            vel_ref.at[:, :, :, lanes], S.at[pl.ds(1, 3), pl.ds(2, nx), h, cols, :], own_sem.at[2 * h + 1]))
    for c in own:
        c.start()

    barrier = pltpu.get_barrier_semaphore()

    def greet(ax, az):
        pl.semaphore_signal(barrier, inc=1, device_id=(ax, az), device_id_type=MESH_ID)

    for d in range(1, n_az):
        greet(me_ax, lax.rem(me_az + d, n_az))

    @pl.when(has_lo)
    def _():
        for d in range(n_az):
            greet(me_ax - 1, lax.rem(me_az + d, n_az))

    @pl.when(has_hi)
    def _():
        for d in range(n_az):
            greet(me_ax + 1, lax.rem(me_az + d, n_az))

    peers = n_az - 1 + jnp.where(has_lo, n_az, 0) + jnp.where(has_hi, n_az, 0)
    pl.semaphore_wait(barrier, peers)

    def halo(kind, src_rows, src_cols, dst_rows, dst_cols, target):
        copies = []
        for h in range(nh):
            lanes = pl.ds(h * LANES, LANES)
            copies.append(pltpu.make_async_remote_copy(
                src_ref=rho_ref.at[src_rows, src_cols, lanes],
                dst_ref=S.at[0, dst_rows, h, dst_cols, :],
                send_sem=halo_send.at[kind, 2 * h], recv_sem=halo_recv.at[kind, 2 * h],
                device_id=target, device_id_type=MESH_ID))
            copies.append(pltpu.make_async_remote_copy(
                src_ref=vel_ref.at[:, src_rows, src_cols, lanes],
                dst_ref=S.at[pl.ds(1, 3), dst_rows, h, dst_cols, :],
                send_sem=halo_send.at[kind, 2 * h + 1], recv_sem=halo_recv.at[kind, 2 * h + 1],
                device_id=target, device_id_type=MESH_ID))
        return copies

    def planes(kind, src, dst, target):
        def cells(at, rows, first, count):
            return halo(kind + at, pl.ds(src + rows[0], rows[1]), pl.ds(first, count),
                        pl.ds(dst + rows[0], rows[1]), pl.ds(EDGE + first, count), target)

        near_row = nx - 1 - src if src else 0
        inner = nt - 2 * SUB
        return (
            cells(0, (0, 2), 0, SUB) + cells(1, (0, 2), nt - SUB, SUB),
            cells(2, (near_row, 1), SUB, inner),
            cells(3, (1 - near_row, 1), SUB, inner),
        )

    up = planes(0, nx - 2, 0, (me_ax + 1, me_az))
    down = planes(4, 0, nx + 2, (me_ax - 1, me_az))
    around = halo(8, pl.ds(0, nx), pl.ds(nt - SUB, SUB), pl.ds(2, nx), pl.ds(EDGE - SUB, SUB), (me_ax, right))
    around += halo(9, pl.ds(0, nx), pl.ds(0, SUB), pl.ds(2, nx), pl.ds(EDGE + nt, SUB), (me_ax, left))

    for step in range(3):
        @pl.when(has_hi)
        def _():
            for c in up[step]:
                c.start()

        @pl.when(has_lo)
        def _():
            for c in down[step]:
                c.start()

        if step == 0:
            for c in around:
                c.start()

    def corner(slot, row):
        rows = pl.ds(row, 2)
        return [
            pltpu.make_async_remote_copy(
                src_ref=S.at[:, rows, :, pl.ds(EDGE + nt - SUB, SUB), :],
                dst_ref=S.at[:, rows, :, pl.ds(EDGE - SUB, SUB), :],
                send_sem=corner_send.at[slot, 0], recv_sem=corner_recv.at[slot, 0],
                device_id=(me_ax, right), device_id_type=MESH_ID),
            pltpu.make_async_remote_copy(
                src_ref=S.at[:, rows, :, pl.ds(EDGE, SUB), :],
                dst_ref=S.at[:, rows, :, pl.ds(EDGE + nt, SUB), :],
                send_sem=corner_send.at[slot, 1], recv_sem=corner_recv.at[slot, 1],
                device_id=(me_ax, left), device_id_type=MESH_ID),
        ]

    lo_corner, hi_corner = corner(0, 0), corner(1, nx + 2)

    def receive(step):
        @pl.when(has_lo)
        def _():
            for c in up[step]:
                c.wait_recv()
            for c in lo_corner:
                c.start() if step == 0 else c.wait() if step == 1 else None

        @pl.when(has_hi)
        def _():
            for c in down[step]:
                c.wait_recv()
            for c in hi_corner:
                c.start() if step == 0 else c.wait() if step == 1 else None

    def low(r):
        return jnp.maximum(r - 1, jnp.where(has_lo, -2, 0))

    def high(r):
        return jnp.minimum(r + 1, jnp.where(has_hi, nx + 1, nx - 1))

    def sweep(first, stride, count, tiles, body):
        tiles = tiles // body.size

        def step(at, carry):
            r = first + stride * (at // tiles)
            body(r, lax.rem(at, tiles))
            return carry

        lax.fori_loop(0, count * tiles, step, 0)

    wide = nt // SUB + 2

    def blocked(name, extent):
        size = math.gcd(BLOCKS[name], extent)

        def mark(body):
            body.size = size
            return body

        return size * SUB, mark

    def spread(values, rows):
        return jnp.concatenate([values] * (rows // SUB), axis=1)

    def near(ref, lead, row, col, shift, n):
        return ref[lead, row, :, pl.ds(col + shift, n), :]

    def tile(ref, lead, row, col, n):
        return ref[lead, row, :, pl.ds(pl.multiple_of(col, SUB), n), :]

    def put(ref, lead, row, col, value):
        ref[lead, row, :, pl.ds(pl.multiple_of(col, SUB), value.shape[1]), :] = value

    def first_pass(with_pairs):
        n, mark = blocked("first", wide)

        @mark
        def body(r, t):
            c = (EDGE - SUB) + t * n
            rows = (low(r) + 2, r + 2, high(r) + 2)
            rho = [tile(S, 0, q, c, n) for q in rows]
            vel = [[tile(S, 1 + a, q, c, n) for a in range(3)] for q in rows]
            inv_r, az_scale, width = (spread(geo_ref[g], n) for g in (0, 1, 2))
            dx = [vel[2][a] - vel[0][a] for a in range(3)]
            dr = [rise(vel[1][a]) * (0.5 / STEP_RADIAL) for a in range(3)]
            dt = [(near(S, 1 + a, r + 2, c, 1, n) - near(S, 1 + a, r + 2, c, -1, n)) * az_scale for a in range(3)]
            dev, size = strain(dx, dr, dt, vel[1][1], vel[1][2], inv_r)
            scale = rho[1] * width * size
            for a in range(6):
                put(M, a, r + 1, c, scale * dev[a])
            mom = [[rho[q] * vel[q][a] for a in range(3)] for q in range(3)]
            put(H, 0, r + 1, c, (rho[0] + rho[1]) + (rho[1] + rho[2]))
            for a in range(3):
                put(H, 1 + a, r + 1, c, (mom[0][a] + mom[1][a]) + (mom[1][a] + mom[2][a]))
            if with_pairs:
                for at, (a, b) in enumerate(PAIRS):
                    p = [mom[q][a] * vel[q][b] for q in range(3)]
                    put(PX, at, r, c, (p[0] + p[1]) + (p[1] + p[2]))
        return body

    def smooth(ref, lead, row, c, n):
        mid_value = tile(ref, lead, row, c, n)
        s = (near(ref, lead, row, c, -1, n) + near(ref, lead, row, c, 1, n)) + (mid_value + mid_value)
        return ((before(s) + after(s)) + (s + s)) * (1.0 / 64.0)

    n_hat, mark_hat = blocked("hat", wide)

    @mark_hat
    def hat_pass(r, t):
        n = n_hat
        c = (EDGE - SUB) + t * n
        hat = [smooth(H, a, r + 1, c, n) for a in range(4)]
        inv = 1.0 / hat[0]
        for a in range(4):
            put(HM, a, r + 1, c, hat[a])
        for a in range(3):
            put(V, a, r + 1, c, hat[1 + a] * inv)

    n_model, mark_model = blocked("model", wide)

    @mark_model
    def model_pass(r, t):
        n = n_model
        c = (EDGE - SUB) + t * n
        for a in range(6):
            m = tile(M, a, r + 1, c, n)
            put(MX, a, r, c, (tile(M, a, low(r) + 1, c, n) + m) + (m + tile(M, a, high(r) + 1, c, n)))

    n_closure, mark_closure = blocked("closure", nt // SUB)

    @mark_closure
    def closure_pass(r, t):
        n = n_closure
        c = EDGE + t * n
        inv_r, az_scale, width4 = (spread(geo_ref[g], n) for g in (0, 1, 3))
        hv = [tile(V, a, r + 1, c, n) for a in range(3)]
        dx = [tile(V, a, high(r) + 1, c, n) - tile(V, a, low(r) + 1, c, n) for a in range(3)]
        dr = [rise(hv[a]) * (0.5 / STEP_RADIAL) for a in range(3)]
        dt = [(near(V, a, r + 1, c, 1, n) - near(V, a, r + 1, c, -1, n)) * az_scale for a in range(3)]
        dev, size = strain(dx, dr, dt, hv[1], hv[2], inv_r)
        scale = width4 * tile(HM, 0, r + 1, c, n) * size
        hm = [tile(HM, 1 + a, r + 1, c, n) for a in range(3)]
        lm, mm = [], []
        for at, (a, b) in enumerate(PAIRS):
            mixed = scale * dev[at] - smooth(MX, at, r, c, n)
            leonard = smooth(PX, at, r, c, n) - hm[a] * hv[b]
            lm.append(leonard * mixed)
            mm.append(mixed * mixed)
        for q, terms in enumerate((lm, mm)):
            cells = (terms[0] + terms[1] + terms[2]) + 2.0 * (terms[3] + terms[4] + terms[5])
            ACC[r, q] += sum(cells[:, s:s + SUB] for s in range(0, n, SUB))

    ACC[...] = jnp.zeros_like(ACC)
    for c in own:
        c.wait()
    for c in around:
        c.wait_recv()
    sweep(1, 1, nx - 2, wide, first_pass(True))
    sweep(1, 1, nx - 2, wide, hat_pass)
    receive(0)
    receive(1)
    sweep(0, nx - 1, 2, wide, first_pass(True))
    sweep(0, nx - 1, 2, wide, hat_pass)
    sweep(1, 1, nx - 2, wide, model_pass)
    sweep(1, 1, nx - 2, nt // SUB, closure_pass)
    receive(2)
    sweep(-1, nx + 1, 2, wide, first_pass(False))
    sweep(-1, nx + 1, 2, wide, hat_pass)
    sweep(0, nx - 1, 2, wide, model_pass)
    sweep(0, nx - 1, 2, nt // SUB, closure_pass)

    for r in range(nx):
        for q in range(2):
            for h in range(nh):
                row = jnp.sum(ACC[r, q, h], axis=0, keepdims=True)
                part[r, pl.ds(q * nh + h, 1), :] = row
                rec[me_az, r, pl.ds(q * nh + h, 1), :] = row

    def share(kind, d, src, dst, ax):
        return pltpu.make_async_remote_copy(
            src_ref=src, dst_ref=dst.at[me_az],
            send_sem=sum_send.at[kind, d], recv_sem=sum_recv.at[kind, d],
            device_id=(ax, lax.rem(me_az + d, n_az)), device_id_type=MESH_ID)

    to_hi = [share(1, d, part.at[nx - 1], rec_lo, me_ax + 1) for d in range(n_az)]
    to_lo = [share(2, d, part.at[0], rec_hi, me_ax - 1) for d in range(n_az)]
    across = [share(0, d, part, rec, me_ax) for d in range(1, n_az)]

    @pl.when(has_hi)
    def _():
        for c in to_hi:
            c.start()

    @pl.when(has_lo)
    def _():
        for c in to_lo:
            c.start()

    for c in across:
        c.start()

    def ratio(sums):
        lm, mm = sums[:nh], sums[nh:]
        return -0.5 * (lm * (1.0 / azimuth_cells)) / (mm * (1.0 / azimuth_cells) + TINY)

    def total(ref):
        sums = ref[0]
        for d in range(1, n_az):
            sums = sums + ref[d]
        return sums

    def keep(row, value):
        for h in range(nh):
            CS[row, h] = jnp.broadcast_to(-2.0 * value[h:h + 1], (SUB, LANES))

    for c in across:
        c.wait_recv()
    for r in range(nx):
        value = ratio(total(rec.at[:, r]))
        keep(r + 1, value)
        for h in range(nh):
            coef_ref[pl.ds(r, 1), pl.ds(h * LANES, LANES)] = value[h:h + 1]

    n_flux, mark_flux = blocked("flux", nt // SUB)

    @mark_flux
    def flux_pass(r, t):
        n = n_flux
        c = EDGE + t * n
        inv_r, az_scale, radius, back, radius2, back2 = (spread(geo_ref[g], n) for g in (0, 1, 4, 5, 6, 7))
        lo, hi = low(r) + 1, high(r) + 1
        here, below, above = (spread(CS[q], n) for q in (r + 1, lo, hi))

        def axial(a):
            return above * tile(M, a, hi, c, n) - below * tile(M, a, lo, c, n)

        def around_of(a):
            return (near(M, a, r + 1, c, 1, n) - near(M, a, r + 1, c, -1, n)) * turn

        turn = here * az_scale
        once = here * radius
        d_xr = rise(once * tile(M, 3, r + 1, c, n)) * back
        d_rr = rise(once * tile(M, 1, r + 1, c, n)) * back
        d_rt = rise(here * radius2 * tile(M, 5, r + 1, c, n)) * back2
        out = (
            axial(0) + d_xr + around_of(4),
            axial(3) + d_rr + around_of(5) - here * tile(M, 2, r + 1, c, n) * inv_r,
            axial(4) + d_rt + around_of(2),
        )
        rows = pl.ds(pl.multiple_of(t * n, SUB), n)
        for a in range(3):
            for h in range(nh):
                flux_ref[a, r, rows, pl.ds(h * LANES, LANES)] = out[a][h]

    sweep(1, 1, nx - 2, nt // SUB, flux_pass)

    @pl.when(has_lo)
    def _():
        for c in to_hi:
            c.wait_recv()
        keep(0, ratio(total(rec_lo)))

    @pl.when(has_hi)
    def _():
        for c in to_lo:
            c.wait_recv()
        keep(nx + 1, ratio(total(rec_hi)))

    sweep(0, nx - 1, 2, nt // SUB, flux_pass)

    for c in across + around:
        c.wait_send()

    @pl.when(has_hi)
    def _():
        for c in up[0] + up[1] + up[2] + to_hi:
            c.wait_send()

    @pl.when(has_lo)
    def _():
        for c in down[0] + down[1] + down[2] + to_lo:
            c.wait_send()


def hand_over(flux_in, coef_in, flux_out, coef_out, flux_buf, coef_buf, sems):
    count = flux_in.shape[0]
    pieces = [(flux_in.at[a], flux_buf.at[a], flux_out.at[a]) for a in range(count)]
    pieces.append((coef_in, coef_buf, coef_out))
    take = [pltpu.make_async_copy(a, b, sems.at[0, at]) for at, (a, b, _) in enumerate(pieces)]
    give = [pltpu.make_async_copy(b, c, sems.at[1, at]) for at, (_, b, c) in enumerate(pieces)]
    for c in take:
        c.start()
    for arrive, leave in zip(take, give):
        arrive.wait()
        leave.start()
    for c in give:
        c.wait()


def shards(n_ax, n_az, density, velocity):
    nx, nt, radial = density.shape
    nh = radial // LANES
    cols = nt + 2 * EDGE
    geo = jnp.asarray(geometry(radial, nt * n_az))

    def field(count, rows):
        return pltpu.VMEM((count, rows, nh, cols, LANES), jnp.float32)

    dma = pltpu.SemaphoreType.DMA
    flux, coef = pl.pallas_call(
        functools.partial(kernel, n_ax, n_az, nx, nt, nh),
        out_shape=(
            jax.ShapeDtypeStruct(velocity.shape, jnp.float32),
            jax.ShapeDtypeStruct((nx, radial), jnp.float32),
        ),
        in_specs=[
            pl.BlockSpec(memory_space=pl.ANY),
            pl.BlockSpec(memory_space=pl.ANY),
            pl.BlockSpec(memory_space=pltpu.VMEM),
        ],
        out_specs=(
            pl.BlockSpec(memory_space=pltpu.VMEM),
            pl.BlockSpec(memory_space=pltpu.VMEM),
        ),
        scratch_shapes=[
            field(4, nx + 4),
            field(6, nx + 2),
            field(4, nx + 2),
            field(3, nx + 2),
            field(4, nx + 2),
            field(6, nx),
            field(6, nx),
            pltpu.VMEM((nx, 2, nh, SUB, LANES), jnp.float32),
            pltpu.VMEM((nx, 2 * nh, LANES), jnp.float32),
            pltpu.VMEM((n_az, nx, 2 * nh, LANES), jnp.float32),
            pltpu.VMEM((n_az, 2 * nh, LANES), jnp.float32),
            pltpu.VMEM((n_az, 2 * nh, LANES), jnp.float32),
            pltpu.VMEM((nx + 2, nh, SUB, LANES), jnp.float32),
            dma((2 * nh,)),
            dma((10, 2 * nh)),
            dma((10, 2 * nh)),
            dma((2, 2)),
            dma((2, 2)),
            dma((3, n_az)),
            dma((3, n_az)),
        ],
        compiler_params=pltpu.CompilerParams(collective_id=0, has_side_effects=True),
        name="closure",
    )(density, velocity, geo)
    anywhere = pl.BlockSpec(memory_space=pl.ANY)
    return pl.pallas_call(
        hand_over,
        out_shape=(
            jax.ShapeDtypeStruct(flux.shape, jnp.float32),
            jax.ShapeDtypeStruct(coef.shape, jnp.float32),
        ),
        in_specs=[anywhere, anywhere],
        out_specs=(anywhere, anywhere),
        scratch_shapes=[
            pltpu.VMEM(flux.shape, jnp.float32),
            pltpu.VMEM(coef.shape, jnp.float32),
            dma((2, flux.shape[0] + 1)),
        ],
        name="hand_over",
    )(flux, coef)


def solution(mesh):
    in_specs = (P("ax", "az", None), P(None, "ax", "az", None))
    out_specs = (P(None, "ax", "az", None), P("ax", None))
    body = functools.partial(shards, mesh.shape["ax"], mesh.shape["az"])
    return jax.shard_map(body, mesh=mesh, in_specs=in_specs, out_specs=out_specs, check_vma=False)
```

```python
import functools
import math

import jax
import jax.numpy as jnp
import numpy as np
from jax import lax
from jax.experimental import pallas as pl
from jax.experimental.pallas import tpu as pltpu
from jax.sharding import PartitionSpec as P

STEP_AXIAL = 0.5
STEP_RADIAL = 0.25
INNER_RADIUS = 10.0
FILTER_RATIO = 2.0
TINY = 1e-06
PAIRS = ((0, 0), (1, 1), (2, 2), (0, 1), (0, 2), (1, 2))
LANES = 128
SUB = 8
BLOCKS = {"first": 5, "hat": 10, "model": 10, "closure": 4, "flux": 4}
EDGE = 16
MESH_ID = pl.DeviceIdType.MESH


def geometry(radial, azimuth_cells):
    radius = INNER_RADIUS + (np.arange(radial, dtype=np.float64) + 0.5) * STEP_RADIAL
    angle = 2.0 * math.pi / azimuth_cells
    width = (STEP_AXIAL * STEP_RADIAL * angle * radius) ** (2.0 / 3.0)
    rows = np.stack(
        [
            1.0 / radius,
            0.5 / (radius * angle),
            width,
            FILTER_RATIO**2 * width,
            radius,
            0.5 / STEP_RADIAL / radius,
            radius * radius,
            0.5 / STEP_RADIAL / (radius * radius),
        ]
    ).astype(np.float32)
    rows = rows.reshape(rows.shape[0], radial // LANES, 1, LANES)
    return np.ascontiguousarray(np.broadcast_to(rows, rows.shape[:2] + (SUB, LANES)))


def before(x):
    lane = lax.broadcasted_iota(jnp.int32, x.shape, x.ndim - 1)
    y = pltpu.roll(x, 1, x.ndim - 1)
    fill = jnp.concatenate([x[:1], y[:-1]], axis=0)
    return jnp.where(lane == 0, fill, y)


def after(x):
    lane = lax.broadcasted_iota(jnp.int32, x.shape, x.ndim - 1)
    y = pltpu.roll(x, LANES - 1, x.ndim - 1)
    fill = jnp.concatenate([y[1:], x[-1:]], axis=0)
    return jnp.where(lane == LANES - 1, fill, y)


def rise(x):
    return after(x) - before(x)


def strain(dx, dr, dt, ur, ut, inv_r):
    s_xx, s_rr = dx[0], dr[1]
    s_tt = dt[2] + ur * inv_r
    s_xr = 0.5 * (dr[0] + dx[1])
    s_xt = 0.5 * (dt[0] + dx[2])
    s_rt = 0.5 * (dt[1] + dr[2] - ut * inv_r)
    size = jnp.sqrt(
        2.0
        * (
            s_xx * s_xx
            + s_rr * s_rr
            + s_tt * s_tt
            + 2.0 * (s_xr * s_xr + s_xt * s_xt + s_rt * s_rt)
        )
    )
    third = (s_xx + s_rr + s_tt) * (1.0 / 3.0)
    return (s_xx - third, s_rr - third, s_tt - third, s_xr, s_xt, s_rt), size


def kernel(
    n_ax, n_az, nx, nt, nh, relays,
    rho_ref, vel_ref, geo_ref, flux_ref, coef_ref,
    S, M, H, V, HM, PX, MX, ACC, part, rec, rec_lo, rec_hi, CS, R,
    own_sem, halo_send, halo_recv, corner_send, corner_recv, sum_send, sum_recv,
    relay_send, relay_recv, pass_send,
):
    me_ax, me_az = lax.axis_index("ax"), lax.axis_index("az")
    left, right = lax.rem(me_az + n_az - 1, n_az), lax.rem(me_az + 1, n_az)
    has_lo, has_hi = me_ax > 0, me_ax < n_ax - 1
    azimuth_cells = nt * n_az

    own = []
    for h in range(nh):
        lanes = pl.ds(h * LANES, LANES)
        cols = pl.ds(EDGE, nt)
        own.append(pltpu.make_async_copy(
            rho_ref.at[:, :, lanes], S.at[0, pl.ds(2, nx), h, cols, :], own_sem.at[2 * h]))
        own.append(pltpu.make_async_copy(
            vel_ref.at[:, :, :, lanes], S.at[pl.ds(1, 3), pl.ds(2, nx), h, cols, :], own_sem.at[2 * h + 1]))
    for c in own:
        c.start()

    barrier = pltpu.get_barrier_semaphore()

    def greet(ax, az):
        pl.semaphore_signal(barrier, inc=1, device_id=(ax, az), device_id_type=MESH_ID)

    for d in range(1, n_az):
        greet(me_ax, lax.rem(me_az + d, n_az))

    @pl.when(has_lo)
    def _():
        for d in range(n_az):
            greet(me_ax - 1, lax.rem(me_az + d, n_az))

    @pl.when(has_hi)
    def _():
        for d in range(n_az):
            greet(me_ax + 1, lax.rem(me_az + d, n_az))

    peers = n_az - 1 + jnp.where(has_lo, n_az, 0) + jnp.where(has_hi, n_az, 0)
    if relays:
        @pl.when(me_ax > 1)
        def _():
            greet(me_ax - 2, me_az)

        @pl.when(me_ax < n_ax - 2)
        def _():
            greet(me_ax + 2, me_az)

        peers = peers + jnp.where(me_ax > 1, 1, 0) + jnp.where(me_ax < n_ax - 2, 1, 0)
    pl.semaphore_wait(barrier, peers)

    def halo(kind, src_rows, src_cols, dst_rows, dst_cols, target):
        copies = []
        for h in range(nh):
            lanes = pl.ds(h * LANES, LANES)
            copies.append(pltpu.make_async_remote_copy(
                src_ref=rho_ref.at[src_rows, src_cols, lanes],
                dst_ref=S.at[0, dst_rows, h, dst_cols, :],
                send_sem=halo_send.at[kind, 2 * h], recv_sem=halo_recv.at[kind, 2 * h],
                device_id=target, device_id_type=MESH_ID))
            copies.append(pltpu.make_async_remote_copy(
                src_ref=vel_ref.at[:, src_rows, src_cols, lanes],
                dst_ref=S.at[pl.ds(1, 3), dst_rows, h, dst_cols, :],
                send_sem=halo_send.at[kind, 2 * h + 1], recv_sem=halo_recv.at[kind, 2 * h + 1],
                device_id=target, device_id_type=MESH_ID))
        return copies

    def planes(kind, src, dst, target):
        def cells(at, rows, first, count):
            return halo(kind + at, pl.ds(src + rows[0], rows[1]), pl.ds(first, count),
                        pl.ds(dst + rows[0], rows[1]), pl.ds(EDGE + first, count), target)

        near_row = nx - 1 - src if src else 0
        return (
            cells(0, (0, 2), 0, SUB) + cells(1, (0, 2), nt - SUB, SUB),
            cells(2, (near_row, 1), SUB, span),
            cells(3, (near_row, 1), SUB + span, span),
            cells(4, (1 - near_row, 1), SUB, span),
            cells(5, (1 - near_row, 1), SUB + span, span),
        )

    span = nt // 2 - SUB
    up = planes(0, nx - 2, 0, (me_ax + 1, me_az))
    down = planes(6, 0, nx + 2, (me_ax - 1, me_az))
    around = halo(12, pl.ds(0, nx), pl.ds(nt - SUB, SUB), pl.ds(2, nx), pl.ds(EDGE - SUB, SUB), (me_ax, right))
    around += halo(13, pl.ds(0, nx), pl.ds(0, SUB), pl.ds(2, nx), pl.ds(EDGE + nt, SUB), (me_ax, left))

    pair, odd = me_ax // 2, lax.rem(me_ax, 2)
    is_odd, is_even = odd == 1, odd == 0
    rank_of = {5: 0, 4: 1, 3: 2}
    sent = jnp.where(is_odd, n_ax // 2 - 1 - pair, pair)
    passed = jnp.where(is_odd, pair, n_ax // 2 - 1 - pair)

    def relay(piece):
        rank, copies = rank_of[piece], []
        row = jnp.where(is_odd, nx - 1, 0) if piece == 3 else jnp.where(is_odd, nx - 2, 1)
        first = SUB + (0 if piece == 4 else span)
        to = (me_ax + 1 - 2 * odd, me_az)
        on = (me_ax + 2 - 4 * odd, me_az)
        land = jnp.where(is_odd, nx + 2, 1) if piece == 3 else jnp.where(is_odd, nx + 3, 0)
        kind = piece + 6 * odd
        onward = []
        for h in range(nh):
            lanes = pl.ds(h * LANES, LANES)
            for q, src, lead in (
                (2 * h, rho_ref.at[pl.ds(row, 1), pl.ds(first, span), lanes], 0),
                (2 * h + 1, vel_ref.at[:, pl.ds(row, 1), pl.ds(first, span), lanes], pl.ds(1, 3)),
            ):
                copies.append(pltpu.make_async_remote_copy(
                    src_ref=src, dst_ref=R.at[rank, lead, :, h],
                    send_sem=relay_send.at[rank, q], recv_sem=relay_recv.at[rank, q],
                    device_id=to, device_id_type=MESH_ID))
                onward.append(pltpu.make_async_remote_copy(
                    src_ref=R.at[rank, lead, :, h],
                    dst_ref=S.at[lead, pl.ds(land, 1), h, pl.ds(EDGE + first, span), :],
                    send_sem=pass_send.at[rank, q], recv_sem=halo_recv.at[kind, q],
                    device_id=on, device_id_type=MESH_ID))
        return copies, onward

    relayed = {piece: relay(piece) for piece in rank_of} if relays else {}

    def sends_up(piece):
        return has_hi & (is_even | (sent <= rank_of[piece])) if piece in relayed else has_hi

    def sends_down(piece):
        return has_lo & (is_odd | (sent <= rank_of[piece])) if piece in relayed else has_lo

    def send_relay(piece):
        if piece in relayed:
            @pl.when(sent > rank_of[piece])
            def _():
                for c in relayed[piece][0]:
                    c.start()

    def pass_on(piece):
        if piece in relayed:
            @pl.when(passed > rank_of[piece])
            def _():
                for got, c in zip(*relayed[piece]):
                    got.wait_recv()
                    c.start()

    for piece in range(5 + 1):
        at = max(piece - 1, 0)
        if piece == 1:
            for c in around:
                c.start()
            continue
        if piece == 3:
            send_relay(3)
        if piece == 4:
            send_relay(4)
            send_relay(5)

        @pl.when(sends_up(piece))
        def _():
            for c in up[at]:
                c.start()

        @pl.when(sends_down(piece))
        def _():
            for c in down[at]:
                c.start()

    def corner(slot, row):
        rows = pl.ds(row, 2)
        return [
            pltpu.make_async_remote_copy(
                src_ref=S.at[:, rows, :, pl.ds(EDGE + nt - SUB, SUB), :],
                dst_ref=S.at[:, rows, :, pl.ds(EDGE - SUB, SUB), :],
                send_sem=corner_send.at[slot, 0], recv_sem=corner_recv.at[slot, 0],
                device_id=(me_ax, right), device_id_type=MESH_ID),
            pltpu.make_async_remote_copy(
                src_ref=S.at[:, rows, :, pl.ds(EDGE, SUB), :],
                dst_ref=S.at[:, rows, :, pl.ds(EDGE + nt, SUB), :],
                send_sem=corner_send.at[slot, 1], recv_sem=corner_recv.at[slot, 1],
                device_id=(me_ax, left), device_id_type=MESH_ID),
        ]

    lo_corner, hi_corner = corner(0, 0), corner(1, nx + 2)

    def groups(flow):
        return flow[0], flow[1] + flow[2], flow[3] + flow[4]

    def receive(step):
        @pl.when(has_lo)
        def _():
            for c in groups(up)[step]:
                c.wait_recv()
            for c in lo_corner:
                c.start() if step == 0 else c.wait() if step == 1 else None

        @pl.when(has_hi)
        def _():
            for c in groups(down)[step]:
                c.wait_recv()
            for c in hi_corner:
                c.start() if step == 0 else c.wait() if step == 1 else None

    def low(r):
        return jnp.maximum(r - 1, jnp.where(has_lo, -2, 0))

    def high(r):
        return jnp.minimum(r + 1, jnp.where(has_hi, nx + 1, nx - 1))

    def sweep(first, stride, count, tiles, body):
        tiles = tiles // body.size

        def step(at, carry):
            r = first + stride * (at // tiles)
            body(r, lax.rem(at, tiles))
            return carry

        lax.fori_loop(0, count * tiles, step, 0)

    wide = nt // SUB + 2

    def blocked(name, extent):
        size = math.gcd(BLOCKS[name], extent)

        def mark(body):
            body.size = size
            return body

        return size * SUB, mark

    def spread(values, rows):
        return jnp.concatenate([values] * (rows // SUB), axis=1)

    def near(ref, lead, row, col, shift, n):
        return ref[lead, row, :, pl.ds(col + shift, n), :]

    def tile(ref, lead, row, col, n):
        return ref[lead, row, :, pl.ds(pl.multiple_of(col, SUB), n), :]

    def put(ref, lead, row, col, value):
        ref[lead, row, :, pl.ds(pl.multiple_of(col, SUB), value.shape[1]), :] = value

    def first_pass(with_pairs):
        n, mark = blocked("first", wide)

        @mark
        def body(r, t):
            c = (EDGE - SUB) + t * n
            rows = (low(r) + 2, r + 2, high(r) + 2)
            rho = [tile(S, 0, q, c, n) for q in rows]
            vel = [[tile(S, 1 + a, q, c, n) for a in range(3)] for q in rows]
            inv_r, az_scale, width = (spread(geo_ref[g], n) for g in (0, 1, 2))
            dx = [vel[2][a] - vel[0][a] for a in range(3)]
            dr = [rise(vel[1][a]) * (0.5 / STEP_RADIAL) for a in range(3)]
            dt = [(near(S, 1 + a, r + 2, c, 1, n) - near(S, 1 + a, r + 2, c, -1, n)) * az_scale for a in range(3)]
            dev, size = strain(dx, dr, dt, vel[1][1], vel[1][2], inv_r)
            scale = rho[1] * width * size
            for a in range(6):
                put(M, a, r + 1, c, scale * dev[a])
            mom = [[rho[q] * vel[q][a] for a in range(3)] for q in range(3)]
            put(H, 0, r + 1, c, (rho[0] + rho[1]) + (rho[1] + rho[2]))
            for a in range(3):
                put(H, 1 + a, r + 1, c, (mom[0][a] + mom[1][a]) + (mom[1][a] + mom[2][a]))
            if with_pairs:
                for at, (a, b) in enumerate(PAIRS):
                    p = [mom[q][a] * vel[q][b] for q in range(3)]
                    put(PX, at, r, c, (p[0] + p[1]) + (p[1] + p[2]))
        return body

    def smooth(ref, lead, row, c, n):
        mid_value = tile(ref, lead, row, c, n)
        s = (near(ref, lead, row, c, -1, n) + near(ref, lead, row, c, 1, n)) + (mid_value + mid_value)
        return ((before(s) + after(s)) + (s + s)) * (1.0 / 64.0)

    n_hat, mark_hat = blocked("hat", wide)

    @mark_hat
    def hat_pass(r, t):
        n = n_hat
        c = (EDGE - SUB) + t * n
        hat = [smooth(H, a, r + 1, c, n) for a in range(4)]
        inv = 1.0 / hat[0]
        for a in range(4):
            put(HM, a, r + 1, c, hat[a])
        for a in range(3):
            put(V, a, r + 1, c, hat[1 + a] * inv)

    n_model, mark_model = blocked("model", wide)

    @mark_model
    def model_pass(r, t):
        n = n_model
        c = (EDGE - SUB) + t * n
        for a in range(6):
            m = tile(M, a, r + 1, c, n)
            put(MX, a, r, c, (tile(M, a, low(r) + 1, c, n) + m) + (m + tile(M, a, high(r) + 1, c, n)))

    n_closure, mark_closure = blocked("closure", nt // SUB)

    @mark_closure
    def closure_pass(r, t):
        n = n_closure
        c = EDGE + t * n
        inv_r, az_scale, width4 = (spread(geo_ref[g], n) for g in (0, 1, 3))
        hv = [tile(V, a, r + 1, c, n) for a in range(3)]
        dx = [tile(V, a, high(r) + 1, c, n) - tile(V, a, low(r) + 1, c, n) for a in range(3)]
        dr = [rise(hv[a]) * (0.5 / STEP_RADIAL) for a in range(3)]
        dt = [(near(V, a, r + 1, c, 1, n) - near(V, a, r + 1, c, -1, n)) * az_scale for a in range(3)]
        dev, size = strain(dx, dr, dt, hv[1], hv[2], inv_r)
        scale = width4 * tile(HM, 0, r + 1, c, n) * size
        hm = [tile(HM, 1 + a, r + 1, c, n) for a in range(3)]
        lm, mm = [], []
        for at, (a, b) in enumerate(PAIRS):
            mixed = scale * dev[at] - smooth(MX, at, r, c, n)
            leonard = smooth(PX, at, r, c, n) - hm[a] * hv[b]
            lm.append(leonard * mixed)
            mm.append(mixed * mixed)
        for q, terms in enumerate((lm, mm)):
            cells = (terms[0] + terms[1] + terms[2]) + 2.0 * (terms[3] + terms[4] + terms[5])
            ACC[r, q] += sum(cells[:, s:s + SUB] for s in range(0, n, SUB))

    ACC[...] = jnp.zeros_like(ACC)
    for c in own:
        c.wait()
    for c in around:
        c.wait_recv()
    sweep(1, 1, nx - 2, wide, first_pass(True))
    sweep(1, 1, nx - 2, wide, hat_pass)
    receive(0)
    pass_on(3)
    receive(1)
    pass_on(4)
    sweep(0, nx - 1, 2, wide, first_pass(True))
    sweep(0, nx - 1, 2, wide, hat_pass)
    pass_on(5)
    sweep(1, 1, nx - 2, wide, model_pass)
    sweep(1, 1, nx - 2, nt // SUB, closure_pass)
    receive(2)
    sweep(-1, nx + 1, 2, wide, first_pass(False))
    sweep(-1, nx + 1, 2, wide, hat_pass)
    sweep(0, nx - 1, 2, wide, model_pass)
    sweep(0, nx - 1, 2, nt // SUB, closure_pass)

    for r in range(nx):
        for q in range(2):
            for h in range(nh):
                row = jnp.sum(ACC[r, q, h], axis=0, keepdims=True)
                part[r, pl.ds(q * nh + h, 1), :] = row
                rec[me_az, r, pl.ds(q * nh + h, 1), :] = row

    def share(kind, d, src, dst, ax):
        return pltpu.make_async_remote_copy(
            src_ref=src, dst_ref=dst.at[me_az],
            send_sem=sum_send.at[kind, d], recv_sem=sum_recv.at[kind, d],
            device_id=(ax, lax.rem(me_az + d, n_az)), device_id_type=MESH_ID)

    to_hi = [share(1, d, part.at[nx - 1], rec_lo, me_ax + 1) for d in range(n_az)]
    to_lo = [share(2, d, part.at[0], rec_hi, me_ax - 1) for d in range(n_az)]
    across = [share(0, d, part, rec, me_ax) for d in range(1, n_az)]

    @pl.when(has_hi)
    def _():
        for c in to_hi:
            c.start()

    @pl.when(has_lo)
    def _():
        for c in to_lo:
            c.start()

    for c in across:
        c.start()

    def ratio(sums):
        lm, mm = sums[:nh], sums[nh:]
        return -0.5 * (lm * (1.0 / azimuth_cells)) / (mm * (1.0 / azimuth_cells) + TINY)

    def total(ref):
        sums = ref[0]
        for d in range(1, n_az):
            sums = sums + ref[d]
        return sums

    def keep(row, value):
        for h in range(nh):
            CS[row, h] = jnp.broadcast_to(-2.0 * value[h:h + 1], (SUB, LANES))

    for c in across:
        c.wait_recv()
    for r in range(nx):
        value = ratio(total(rec.at[:, r]))
        keep(r + 1, value)
        for h in range(nh):
            coef_ref[pl.ds(r, 1), pl.ds(h * LANES, LANES)] = value[h:h + 1]

    n_flux, mark_flux = blocked("flux", nt // SUB)

    @mark_flux
    def flux_pass(r, t):
        n = n_flux
        c = EDGE + t * n
        inv_r, az_scale, radius, back, radius2, back2 = (spread(geo_ref[g], n) for g in (0, 1, 4, 5, 6, 7))
        lo, hi = low(r) + 1, high(r) + 1
        here, below, above = (spread(CS[q], n) for q in (r + 1, lo, hi))

        def axial(a):
            return above * tile(M, a, hi, c, n) - below * tile(M, a, lo, c, n)

        def around_of(a):
            return (near(M, a, r + 1, c, 1, n) - near(M, a, r + 1, c, -1, n)) * turn

        turn = here * az_scale
        once = here * radius
        d_xr = rise(once * tile(M, 3, r + 1, c, n)) * back
        d_rr = rise(once * tile(M, 1, r + 1, c, n)) * back
        d_rt = rise(here * radius2 * tile(M, 5, r + 1, c, n)) * back2
        out = (
            axial(0) + d_xr + around_of(4),
            axial(3) + d_rr + around_of(5) - here * tile(M, 2, r + 1, c, n) * inv_r,
            axial(4) + d_rt + around_of(2),
        )
        rows = pl.ds(pl.multiple_of(t * n, SUB), n)
        for a in range(3):
            for h in range(nh):
                flux_ref[a, r, rows, pl.ds(h * LANES, LANES)] = out[a][h]

    sweep(1, 1, nx - 2, nt // SUB, flux_pass)

    @pl.when(has_lo)
    def _():
        for c in to_hi:
            c.wait_recv()
        keep(0, ratio(total(rec_lo)))

    @pl.when(has_hi)
    def _():
        for c in to_lo:
            c.wait_recv()
        keep(nx + 1, ratio(total(rec_hi)))

    sweep(0, nx - 1, 2, nt // SUB, flux_pass)

    for c in across + around:
        c.wait_send()

    for piece in (0, 2, 3, 4, 5):
        at = max(piece - 1, 0)

        @pl.when(sends_up(piece))
        def _():
            for c in up[at]:
                c.wait_send()

        @pl.when(sends_down(piece))
        def _():
            for c in down[at]:
                c.wait_send()

    for piece, (copies, onward) in relayed.items():
        @pl.when(sent > rank_of[piece])
        def _():
            for c in copies:
                c.wait_send()

        @pl.when(passed > rank_of[piece])
        def _():
            for c in onward:
                c.wait_send()

    @pl.when(has_hi)
    def _():
        for c in to_hi:
            c.wait_send()

    @pl.when(has_lo)
    def _():
        for c in to_lo:
            c.wait_send()


def hand_over(flux_in, coef_in, flux_out, coef_out, flux_buf, coef_buf, sems):
    count = flux_in.shape[0]
    pieces = [(flux_in.at[a], flux_buf.at[a], flux_out.at[a]) for a in range(count)]
    pieces.append((coef_in, coef_buf, coef_out))
    take = [pltpu.make_async_copy(a, b, sems.at[0, at]) for at, (a, b, _) in enumerate(pieces)]
    give = [pltpu.make_async_copy(b, c, sems.at[1, at]) for at, (_, b, c) in enumerate(pieces)]
    for c in take:
        c.start()
    for arrive, leave in zip(take, give):
        arrive.wait()
        leave.start()
    for c in give:
        c.wait()


def shards(n_ax, n_az, density, velocity):
    nx, nt, radial = density.shape
    nh = radial // LANES
    cols = nt + 2 * EDGE
    relays = n_ax == 8
    geo = jnp.asarray(geometry(radial, nt * n_az))

    def field(count, rows):
        return pltpu.VMEM((count, rows, nh, cols, LANES), jnp.float32)

    dma = pltpu.SemaphoreType.DMA
    flux, coef = pl.pallas_call(
        functools.partial(kernel, n_ax, n_az, nx, nt, nh, relays),
        out_shape=(
            jax.ShapeDtypeStruct(velocity.shape, jnp.float32),
            jax.ShapeDtypeStruct((nx, radial), jnp.float32),
        ),
        in_specs=[
            pl.BlockSpec(memory_space=pl.ANY),
            pl.BlockSpec(memory_space=pl.ANY),
            pl.BlockSpec(memory_space=pltpu.VMEM),
        ],
        out_specs=(
            pl.BlockSpec(memory_space=pltpu.VMEM),
            pl.BlockSpec(memory_space=pltpu.VMEM),
        ),
        scratch_shapes=[
            field(4, nx + 4),
            field(6, nx + 2),
            field(4, nx + 2),
            field(3, nx + 2),
            field(4, nx + 2),
            field(6, nx),
            field(6, nx),
            pltpu.VMEM((nx, 2, nh, SUB, LANES), jnp.float32),
            pltpu.VMEM((nx, 2 * nh, LANES), jnp.float32),
            pltpu.VMEM((n_az, nx, 2 * nh, LANES), jnp.float32),
            pltpu.VMEM((n_az, 2 * nh, LANES), jnp.float32),
            pltpu.VMEM((n_az, 2 * nh, LANES), jnp.float32),
            pltpu.VMEM((nx + 2, nh, SUB, LANES), jnp.float32),
            pltpu.VMEM((3, 4, 1, nh, nt // 2 - SUB, LANES), jnp.float32),
            dma((2 * nh,)),
            dma((14, 2 * nh)),
            dma((14, 2 * nh)),
            dma((2, 2)),
            dma((2, 2)),
            dma((3, n_az)),
            dma((3, n_az)),
            dma((3, 2 * nh)),
            dma((3, 2 * nh)),
            dma((3, 2 * nh)),
        ],
        compiler_params=pltpu.CompilerParams(collective_id=0, has_side_effects=True),
        name="closure",
    )(density, velocity, geo)
    anywhere = pl.BlockSpec(memory_space=pl.ANY)
    return pl.pallas_call(
        hand_over,
        out_shape=(
            jax.ShapeDtypeStruct(flux.shape, jnp.float32),
            jax.ShapeDtypeStruct(coef.shape, jnp.float32),
        ),
        in_specs=[anywhere, anywhere],
        out_specs=(anywhere, anywhere),
        scratch_shapes=[
            pltpu.VMEM(flux.shape, jnp.float32),
            pltpu.VMEM(coef.shape, jnp.float32),
            dma((2, flux.shape[0] + 1)),
        ],
        name="hand_over",
    )(flux, coef)


def solution(mesh):
    in_specs = (P("ax", "az", None), P(None, "ax", "az", None))
    out_specs = (P(None, "ax", "az", None), P("ax", None))
    body = functools.partial(shards, mesh.shape["ax"], mesh.shape["az"])
    return jax.shard_map(body, mesh=mesh, in_specs=in_specs, out_specs=out_specs, check_vma=False)
```

```python
import functools
import math

import jax
import jax.numpy as jnp
import numpy as np
from jax import lax
from jax.experimental import pallas as pl
from jax.experimental.pallas import tpu as pltpu
from jax.sharding import PartitionSpec as P

STEP_AXIAL = 0.5
STEP_RADIAL = 0.25
INNER_RADIUS = 10.0
FILTER_RATIO = 2.0
TINY = 1e-06
PAIRS = ((0, 0), (1, 1), (2, 2), (0, 1), (0, 2), (1, 2))
LANES = 128
SUB = 8
BLOCKS = {"first": 10, "hat": 10, "model": 10, "closure": 8, "flux": 8}
EDGE = 16
MESH_ID = pl.DeviceIdType.MESH


def geometry(radial, azimuth_cells):
    radius = INNER_RADIUS + (np.arange(radial, dtype=np.float64) + 0.5) * STEP_RADIAL
    angle = 2.0 * math.pi / azimuth_cells
    width = (STEP_AXIAL * STEP_RADIAL * angle * radius) ** (2.0 / 3.0)
    rows = np.stack(
        [
            1.0 / radius,
            0.5 / (radius * angle),
            width,
            FILTER_RATIO**2 * width,
            radius,
            0.5 / STEP_RADIAL / radius,
            radius * radius,
            0.5 / STEP_RADIAL / (radius * radius),
        ]
    ).astype(np.float32)
    rows = rows.reshape(rows.shape[0], radial // LANES, 1, LANES)
    return np.ascontiguousarray(np.broadcast_to(rows, rows.shape[:2] + (SUB, LANES)))


def before(x):
    lane = lax.broadcasted_iota(jnp.int32, x.shape, x.ndim - 1)
    y = pltpu.roll(x, 1, x.ndim - 1)
    fill = jnp.concatenate([x[:1], y[:-1]], axis=0)
    return jnp.where(lane == 0, fill, y)


def after(x):
    lane = lax.broadcasted_iota(jnp.int32, x.shape, x.ndim - 1)
    y = pltpu.roll(x, LANES - 1, x.ndim - 1)
    fill = jnp.concatenate([y[1:], x[-1:]], axis=0)
    return jnp.where(lane == LANES - 1, fill, y)


def rise(x):
    return after(x) - before(x)


def strain(dx, dr, dt, ur, ut, inv_r):
    s_xx, s_rr = dx[0], dr[1]
    s_tt = dt[2] + ur * inv_r
    s_xr = 0.5 * (dr[0] + dx[1])
    s_xt = 0.5 * (dt[0] + dx[2])
    s_rt = 0.5 * (dt[1] + dr[2] - ut * inv_r)
    size = jnp.sqrt(
        2.0
        * (
            s_xx * s_xx
            + s_rr * s_rr
            + s_tt * s_tt
            + 2.0 * (s_xr * s_xr + s_xt * s_xt + s_rt * s_rt)
        )
    )
    third = (s_xx + s_rr + s_tt) * (1.0 / 3.0)
    return (s_xx - third, s_rr - third, s_tt - third, s_xr, s_xt, s_rt), size


def kernel(
    n_ax, n_az, nx, nt, nh, relays,
    rho_ref, vel_ref, geo_ref, flux_ref, coef_ref,
    S, M, H, V, HM, PX, MX, ACC, part, rec, rec_lo, rec_hi, CS, R, LE,
    own_sem, halo_send, halo_recv, corner_send, corner_recv, sum_send, sum_recv,
    relay_send, relay_recv, pass_send,
):
    me_ax, me_az = lax.axis_index("ax"), lax.axis_index("az")
    left, right = lax.rem(me_az + n_az - 1, n_az), lax.rem(me_az + 1, n_az)
    has_lo, has_hi = me_ax > 0, me_ax < n_ax - 1
    azimuth_cells = nt * n_az

    own = []
    for h in range(nh):
        lanes = pl.ds(h * LANES, LANES)
        cols = pl.ds(EDGE, nt)
        own.append(pltpu.make_async_copy(
            rho_ref.at[:, :, lanes], S.at[0, pl.ds(2, nx), h, cols, :], own_sem.at[2 * h]))
        own.append(pltpu.make_async_copy(
            vel_ref.at[:, :, :, lanes], S.at[pl.ds(1, 3), pl.ds(2, nx), h, cols, :], own_sem.at[2 * h + 1]))
    for c in own:
        c.start()

    barrier = pltpu.get_barrier_semaphore()

    def greet(ax, az):
        pl.semaphore_signal(barrier, inc=1, device_id=(ax, az), device_id_type=MESH_ID)

    for d in range(1, n_az):
        greet(me_ax, lax.rem(me_az + d, n_az))

    @pl.when(has_lo)
    def _():
        for d in range(n_az):
            greet(me_ax - 1, lax.rem(me_az + d, n_az))

    @pl.when(has_hi)
    def _():
        for d in range(n_az):
            greet(me_ax + 1, lax.rem(me_az + d, n_az))

    peers = n_az - 1 + jnp.where(has_lo, n_az, 0) + jnp.where(has_hi, n_az, 0)
    if relays:
        @pl.when(me_ax > 1)
        def _():
            greet(me_ax - 2, me_az)

        @pl.when(me_ax < n_ax - 2)
        def _():
            greet(me_ax + 2, me_az)

        peers = peers + jnp.where(me_ax > 1, 1, 0) + jnp.where(me_ax < n_ax - 2, 1, 0)
    pl.semaphore_wait(barrier, peers)

    def halo(kind, src_rows, src_cols, dst_rows, dst_cols, target):
        copies = []
        for h in range(nh):
            lanes = pl.ds(h * LANES, LANES)
            copies.append(pltpu.make_async_remote_copy(
                src_ref=rho_ref.at[src_rows, src_cols, lanes],
                dst_ref=S.at[0, dst_rows, h, dst_cols, :],
                send_sem=halo_send.at[kind, 2 * h], recv_sem=halo_recv.at[kind, 2 * h],
                device_id=target, device_id_type=MESH_ID))
            copies.append(pltpu.make_async_remote_copy(
                src_ref=vel_ref.at[:, src_rows, src_cols, lanes],
                dst_ref=S.at[pl.ds(1, 3), dst_rows, h, dst_cols, :],
                send_sem=halo_send.at[kind, 2 * h + 1], recv_sem=halo_recv.at[kind, 2 * h + 1],
                device_id=target, device_id_type=MESH_ID))
        return copies

    def planes(kind, src, dst, target):
        def cells(at, rows, first, count):
            return halo(kind + at, pl.ds(src + rows[0], rows[1]), pl.ds(first, count),
                        pl.ds(dst + rows[0], rows[1]), pl.ds(EDGE + first, count), target)

        near_row = nx - 1 - src if src else 0
        return (
            cells(0, (0, 2), 0, SUB) + cells(1, (0, 2), nt - SUB, SUB),
            cells(2, (near_row, 1), SUB, span),
            cells(3, (near_row, 1), SUB + span, span),
            cells(4, (1 - near_row, 1), SUB, span),
            cells(5, (1 - near_row, 1), SUB + span, span),
        )

    span = nt // 2 - SUB
    up = planes(0, nx - 2, 0, (me_ax + 1, me_az))
    down = planes(6, 0, nx + 2, (me_ax - 1, me_az))
    around = halo(12, pl.ds(0, nx), pl.ds(nt - SUB, SUB), pl.ds(2, nx), pl.ds(EDGE - SUB, SUB), (me_ax, right))
    around += halo(13, pl.ds(0, nx), pl.ds(0, SUB), pl.ds(2, nx), pl.ds(EDGE + nt, SUB), (me_ax, left))

    pair, odd = me_ax // 2, lax.rem(me_ax, 2)
    is_odd, is_even = odd == 1, odd == 0
    rank_of = {5: 0, 4: 1, 3: 2}
    sent = jnp.where(is_odd, n_ax // 2 - 1 - pair, pair)
    passed = jnp.where(is_odd, pair, n_ax // 2 - 1 - pair)

    def relay(piece):
        rank, copies = rank_of[piece], []
        row = jnp.where(is_odd, nx - 1, 0) if piece == 3 else jnp.where(is_odd, nx - 2, 1)
        first = SUB + (0 if piece == 4 else span)
        to = (me_ax + 1 - 2 * odd, me_az)
        on = (me_ax + 2 - 4 * odd, me_az)
        land = jnp.where(is_odd, nx + 2, 1) if piece == 3 else jnp.where(is_odd, nx + 3, 0)
        kind = piece + 6 * odd
        onward = []
        for h in range(nh):
            lanes = pl.ds(h * LANES, LANES)
            for q, src, lead in (
                (2 * h, rho_ref.at[pl.ds(row, 1), pl.ds(first, span), lanes], 0),
                (2 * h + 1, vel_ref.at[:, pl.ds(row, 1), pl.ds(first, span), lanes], pl.ds(1, 3)),
            ):
                copies.append(pltpu.make_async_remote_copy(
                    src_ref=src, dst_ref=R.at[rank, lead, :, h],
                    send_sem=relay_send.at[rank, q], recv_sem=relay_recv.at[rank, q],
                    device_id=to, device_id_type=MESH_ID))
                onward.append(pltpu.make_async_remote_copy(
                    src_ref=R.at[rank, lead, :, h],
                    dst_ref=S.at[lead, pl.ds(land, 1), h, pl.ds(EDGE + first, span), :],
                    send_sem=pass_send.at[rank, q], recv_sem=halo_recv.at[kind, q],
                    device_id=on, device_id_type=MESH_ID))
        return copies, onward

    relayed = {piece: relay(piece) for piece in rank_of} if relays else {}

    def sends_up(piece):
        return has_hi & (is_even | (sent <= rank_of[piece])) if piece in relayed else has_hi

    def sends_down(piece):
        return has_lo & (is_odd | (sent <= rank_of[piece])) if piece in relayed else has_lo

    def send_relay(piece):
        if piece in relayed:
            @pl.when(sent > rank_of[piece])
            def _():
                for c in relayed[piece][0]:
                    c.start()

    def pass_on(piece):
        if piece in relayed:
            @pl.when(passed > rank_of[piece])
            def _():
                for got, c in zip(*relayed[piece]):
                    got.wait_recv()
                    c.start()

    for piece in range(5 + 1):
        at = max(piece - 1, 0)
        if piece == 1:
            for c in around:
                c.start()
            continue
        if piece == 3:
            send_relay(3)
        if piece == 4:
            send_relay(4)
            send_relay(5)

        @pl.when(sends_up(piece))
        def _():
            for c in up[at]:
                c.start()

        @pl.when(sends_down(piece))
        def _():
            for c in down[at]:
                c.start()

    def corner(slot, row):
        rows = pl.ds(row, 2)
        return [
            pltpu.make_async_remote_copy(
                src_ref=S.at[:, rows, :, pl.ds(EDGE + nt - SUB, SUB), :],
                dst_ref=S.at[:, rows, :, pl.ds(EDGE - SUB, SUB), :],
                send_sem=corner_send.at[slot, 0], recv_sem=corner_recv.at[slot, 0],
                device_id=(me_ax, right), device_id_type=MESH_ID),
            pltpu.make_async_remote_copy(
                src_ref=S.at[:, rows, :, pl.ds(EDGE, SUB), :],
                dst_ref=S.at[:, rows, :, pl.ds(EDGE + nt, SUB), :],
                send_sem=corner_send.at[slot, 1], recv_sem=corner_recv.at[slot, 1],
                device_id=(me_ax, left), device_id_type=MESH_ID),
        ]

    lo_corner, hi_corner = corner(0, 0), corner(1, nx + 2)

    def groups(flow):
        return flow[0], flow[1] + flow[2], flow[3] + flow[4]

    def receive(step):
        @pl.when(has_lo)
        def _():
            for c in groups(up)[step]:
                c.wait_recv()
            for c in lo_corner:
                c.start() if step == 0 else c.wait() if step == 1 else None

        @pl.when(has_hi)
        def _():
            for c in groups(down)[step]:
                c.wait_recv()
            for c in hi_corner:
                c.start() if step == 0 else c.wait() if step == 1 else None

    def low(r):
        return jnp.maximum(r - 1, jnp.where(has_lo, -2, 0))

    def high(r):
        return jnp.minimum(r + 1, jnp.where(has_hi, nx + 1, nx - 1))

    def sweep(first, stride, count, tiles, body):
        tiles = tiles // body.size

        def step(at, carry):
            r = first + stride * (at // tiles)
            body(r, lax.rem(at, tiles))
            return carry

        lax.fori_loop(0, count * tiles, step, 0)

    wide = nt // SUB + 2

    def blocked(name, extent):
        size = math.gcd(BLOCKS[name], extent)

        def mark(body):
            body.size = size
            return body

        return size * SUB, mark

    def spread(values, rows):
        return jnp.concatenate([values] * (rows // SUB), axis=1)

    def near(ref, lead, row, col, shift, n):
        return ref[lead, row, :, pl.ds(col + shift, n), :]

    def tile(ref, lead, row, col, n):
        return ref[lead, row, :, pl.ds(pl.multiple_of(col, SUB), n), :]

    def put(ref, lead, row, col, value):
        ref[lead, row, :, pl.ds(pl.multiple_of(col, SUB), value.shape[1]), :] = value

    def first_pass(with_pairs):
        n, mark = blocked("first", wide)

        @mark
        def body(r, t):
            c = (EDGE - SUB) + t * n
            rows = (low(r) + 2, r + 2, high(r) + 2)
            rho = [tile(S, 0, q, c, n) for q in rows]
            vel = [[tile(S, 1 + a, q, c, n) for a in range(3)] for q in rows]
            inv_r, az_scale, width = (spread(geo_ref[g], n) for g in (0, 1, 2))
            dx = [vel[2][a] - vel[0][a] for a in range(3)]
            dr = [rise(vel[1][a]) * (0.5 / STEP_RADIAL) for a in range(3)]
            dt = [(near(S, 1 + a, r + 2, c, 1, n) - near(S, 1 + a, r + 2, c, -1, n)) * az_scale for a in range(3)]
            dev, size = strain(dx, dr, dt, vel[1][1], vel[1][2], inv_r)
            scale = rho[1] * width * size
            for a in range(6):
                put(M, a, r + 1, c, scale * dev[a])
            mom = [[rho[q] * vel[q][a] for a in range(3)] for q in range(3)]
            put(H, 0, r + 1, c, (rho[0] + rho[1]) + (rho[1] + rho[2]))
            for a in range(3):
                put(H, 1 + a, r + 1, c, (mom[0][a] + mom[1][a]) + (mom[1][a] + mom[2][a]))
            if with_pairs:
                for at, (a, b) in enumerate(PAIRS):
                    p = [mom[q][a] * vel[q][b] for q in range(3)]
                    put(PX, at, r, c, (p[0] + p[1]) + (p[1] + p[2]))
        return body

    def smooth(ref, lead, row, c, n):
        mid_value = tile(ref, lead, row, c, n)
        s = (near(ref, lead, row, c, -1, n) + near(ref, lead, row, c, 1, n)) + (mid_value + mid_value)
        return ((before(s) + after(s)) + (s + s)) * (1.0 / 64.0)

    n_hat, mark_hat = blocked("hat", wide)

    @mark_hat
    def hat_pass(r, t):
        n = n_hat
        c = (EDGE - SUB) + t * n
        hat = [smooth(H, a, r + 1, c, n) for a in range(4)]
        inv = 1.0 / hat[0]
        for a in range(4):
            put(HM, a, r + 1, c, hat[a])
        for a in range(3):
            put(V, a, r + 1, c, hat[1 + a] * inv)

    n_model, mark_model = blocked("model", wide)

    @mark_model
    def model_pass(r, t):
        n = n_model
        c = (EDGE - SUB) + t * n
        for a in range(6):
            m = tile(M, a, r + 1, c, n)
            put(MX, a, r, c, (tile(M, a, low(r) + 1, c, n) + m) + (m + tile(M, a, high(r) + 1, c, n)))

    n_leonard, mark_leonard = blocked("closure", nt // SUB)

    @mark_leonard
    def leonard_pass(r, t):
        n = n_leonard
        c = EDGE + t * n
        hv = [tile(V, a, r + 1, c, n) for a in range(3)]
        hm = [tile(HM, 1 + a, r + 1, c, n) for a in range(3)]
        for at, (a, b) in enumerate(PAIRS):
            put(LE, at, r, c, smooth(PX, at, r, c, n) - hm[a] * hv[b])

    n_closure, mark_closure = blocked("closure", nt // SUB)

    @mark_closure
    def closure_pass(r, t):
        n = n_closure
        c = EDGE + t * n
        inv_r, az_scale, width4 = (spread(geo_ref[g], n) for g in (0, 1, 3))
        hv = [tile(V, a, r + 1, c, n) for a in range(3)]
        dx = [tile(V, a, high(r) + 1, c, n) - tile(V, a, low(r) + 1, c, n) for a in range(3)]
        dr = [rise(hv[a]) * (0.5 / STEP_RADIAL) for a in range(3)]
        dt = [(near(V, a, r + 1, c, 1, n) - near(V, a, r + 1, c, -1, n)) * az_scale for a in range(3)]
        dev, size = strain(dx, dr, dt, hv[1], hv[2], inv_r)
        scale = width4 * tile(HM, 0, r + 1, c, n) * size
        lm, mm = [], []
        for at in range(6):
            mixed = scale * dev[at] - smooth(MX, at, r, c, n)
            leonard = tile(LE, at, r, c, n)
            lm.append(leonard * mixed)
            mm.append(mixed * mixed)
        for q, terms in enumerate((lm, mm)):
            cells = (terms[0] + terms[1] + terms[2]) + 2.0 * (terms[3] + terms[4] + terms[5])
            ACC[r, q] += sum(cells[:, s:s + SUB] for s in range(0, n, SUB))

    ACC[...] = jnp.zeros_like(ACC)
    for c in own:
        c.wait()
    for c in around:
        c.wait_recv()
    sweep(1, 1, nx - 2, wide, first_pass(True))
    sweep(1, 1, nx - 2, wide, hat_pass)
    receive(0)
    pass_on(3)
    receive(1)
    pass_on(4)
    sweep(0, nx - 1, 2, wide, first_pass(True))
    sweep(0, nx - 1, 2, wide, hat_pass)
    pass_on(5)
    sweep(0, 1, nx, nt // SUB, leonard_pass)
    sweep(1, 1, nx - 2, wide, model_pass)
    sweep(1, 1, nx - 2, nt // SUB, closure_pass)
    receive(2)
    sweep(-1, nx + 1, 2, wide, first_pass(False))
    sweep(-1, nx + 1, 2, wide, hat_pass)
    sweep(0, nx - 1, 2, wide, model_pass)
    sweep(0, nx - 1, 2, nt // SUB, closure_pass)

    for r in range(nx):
        for q in range(2):
            for h in range(nh):
                row = jnp.sum(ACC[r, q, h], axis=0, keepdims=True)
                part[r, pl.ds(q * nh + h, 1), :] = row
                rec[me_az, r, pl.ds(q * nh + h, 1), :] = row

    def share(kind, d, src, dst, ax):
        return pltpu.make_async_remote_copy(
            src_ref=src, dst_ref=dst.at[me_az],
            send_sem=sum_send.at[kind, d], recv_sem=sum_recv.at[kind, d],
            device_id=(ax, lax.rem(me_az + d, n_az)), device_id_type=MESH_ID)

    to_hi = [share(1, d, part.at[nx - 1], rec_lo, me_ax + 1) for d in range(n_az)]
    to_lo = [share(2, d, part.at[0], rec_hi, me_ax - 1) for d in range(n_az)]
    across = [share(0, d, part, rec, me_ax) for d in range(1, n_az)]

    @pl.when(has_hi)
    def _():
        for c in to_hi:
            c.start()

    @pl.when(has_lo)
    def _():
        for c in to_lo:
            c.start()

    for c in across:
        c.start()

    def ratio(sums):
        lm, mm = sums[:nh], sums[nh:]
        return -0.5 * (lm * (1.0 / azimuth_cells)) / (mm * (1.0 / azimuth_cells) + TINY)

    def total(ref):
        sums = ref[0]
        for d in range(1, n_az):
            sums = sums + ref[d]
        return sums

    def keep(row, value):
        for h in range(nh):
            CS[row, h] = jnp.broadcast_to(-2.0 * value[h:h + 1], (SUB, LANES))

    for c in across:
        c.wait_recv()
    for r in range(nx):
        value = ratio(total(rec.at[:, r]))
        keep(r + 1, value)
        for h in range(nh):
            coef_ref[pl.ds(r, 1), pl.ds(h * LANES, LANES)] = value[h:h + 1]

    n_flux, mark_flux = blocked("flux", nt // SUB)

    @mark_flux
    def flux_pass(r, t):
        n = n_flux
        c = EDGE + t * n
        inv_r, az_scale, radius, back, radius2, back2 = (spread(geo_ref[g], n) for g in (0, 1, 4, 5, 6, 7))
        lo, hi = low(r) + 1, high(r) + 1
        here, below, above = (spread(CS[q], n) for q in (r + 1, lo, hi))

        def axial(a):
            return above * tile(M, a, hi, c, n) - below * tile(M, a, lo, c, n)

        def around_of(a):
            return (near(M, a, r + 1, c, 1, n) - near(M, a, r + 1, c, -1, n)) * turn

        turn = here * az_scale
        once = here * radius
        d_xr = rise(once * tile(M, 3, r + 1, c, n)) * back
        d_rr = rise(once * tile(M, 1, r + 1, c, n)) * back
        d_rt = rise(here * radius2 * tile(M, 5, r + 1, c, n)) * back2
        out = (
            axial(0) + d_xr + around_of(4),
            axial(3) + d_rr + around_of(5) - here * tile(M, 2, r + 1, c, n) * inv_r,
            axial(4) + d_rt + around_of(2),
        )
        rows = pl.ds(pl.multiple_of(t * n, SUB), n)
        for a in range(3):
            for h in range(nh):
                flux_ref[a, r, rows, pl.ds(h * LANES, LANES)] = out[a][h]

    sweep(1, 1, nx - 2, nt // SUB, flux_pass)

    @pl.when(has_lo)
    def _():
        for c in to_hi:
            c.wait_recv()
        keep(0, ratio(total(rec_lo)))

    @pl.when(has_hi)
    def _():
        for c in to_lo:
            c.wait_recv()
        keep(nx + 1, ratio(total(rec_hi)))

    sweep(0, nx - 1, 2, nt // SUB, flux_pass)

    for c in across + around:
        c.wait_send()

    for piece in (0, 2, 3, 4, 5):
        at = max(piece - 1, 0)

        @pl.when(sends_up(piece))
        def _():
            for c in up[at]:
                c.wait_send()

        @pl.when(sends_down(piece))
        def _():
            for c in down[at]:
                c.wait_send()

    for piece, (copies, onward) in relayed.items():
        @pl.when(sent > rank_of[piece])
        def _():
            for c in copies:
                c.wait_send()

        @pl.when(passed > rank_of[piece])
        def _():
            for c in onward:
                c.wait_send()

    @pl.when(has_hi)
    def _():
        for c in to_hi:
            c.wait_send()

    @pl.when(has_lo)
    def _():
        for c in to_lo:
            c.wait_send()


def hand_over(flux_in, coef_in, flux_out, coef_out, flux_buf, coef_buf, sems):
    count = flux_in.shape[0]
    pieces = [(flux_in.at[a], flux_buf.at[a], flux_out.at[a]) for a in range(count)]
    pieces.append((coef_in, coef_buf, coef_out))
    take = [pltpu.make_async_copy(a, b, sems.at[0, at]) for at, (a, b, _) in enumerate(pieces)]
    give = [pltpu.make_async_copy(b, c, sems.at[1, at]) for at, (_, b, c) in enumerate(pieces)]
    for c in take:
        c.start()
    for arrive, leave in zip(take, give):
        arrive.wait()
        leave.start()
    for c in give:
        c.wait()


def shards(n_ax, n_az, density, velocity):
    nx, nt, radial = density.shape
    nh = radial // LANES
    cols = nt + 2 * EDGE
    relays = n_ax == 8
    geo = jnp.asarray(geometry(radial, nt * n_az))

    def field(count, rows):
        return pltpu.VMEM((count, rows, nh, cols, LANES), jnp.float32)

    dma = pltpu.SemaphoreType.DMA
    flux, coef = pl.pallas_call(
        functools.partial(kernel, n_ax, n_az, nx, nt, nh, relays),
        out_shape=(
            jax.ShapeDtypeStruct(velocity.shape, jnp.float32),
            jax.ShapeDtypeStruct((nx, radial), jnp.float32),
        ),
        in_specs=[
            pl.BlockSpec(memory_space=pl.ANY),
            pl.BlockSpec(memory_space=pl.ANY),
            pl.BlockSpec(memory_space=pltpu.VMEM),
        ],
        out_specs=(
            pl.BlockSpec(memory_space=pltpu.VMEM),
            pl.BlockSpec(memory_space=pltpu.VMEM),
        ),
        scratch_shapes=[
            field(4, nx + 4),
            field(6, nx + 2),
            field(4, nx + 2),
            field(3, nx + 2),
            field(4, nx + 2),
            field(6, nx),
            field(6, nx),
            pltpu.VMEM((nx, 2, nh, SUB, LANES), jnp.float32),
            pltpu.VMEM((nx, 2 * nh, LANES), jnp.float32),
            pltpu.VMEM((n_az, nx, 2 * nh, LANES), jnp.float32),
            pltpu.VMEM((n_az, 2 * nh, LANES), jnp.float32),
            pltpu.VMEM((n_az, 2 * nh, LANES), jnp.float32),
            pltpu.VMEM((nx + 2, nh, SUB, LANES), jnp.float32),
            pltpu.VMEM((3, 4, 1, nh, nt // 2 - SUB, LANES), jnp.float32),
            field(6, nx),
            dma((2 * nh,)),
            dma((14, 2 * nh)),
            dma((14, 2 * nh)),
            dma((2, 2)),
            dma((2, 2)),
            dma((3, n_az)),
            dma((3, n_az)),
            dma((3, 2 * nh)),
            dma((3, 2 * nh)),
            dma((3, 2 * nh)),
        ],
        compiler_params=pltpu.CompilerParams(collective_id=0, has_side_effects=True),
        name="closure",
    )(density, velocity, geo)
    anywhere = pl.BlockSpec(memory_space=pl.ANY)
    return pl.pallas_call(
        hand_over,
        out_shape=(
            jax.ShapeDtypeStruct(flux.shape, jnp.float32),
            jax.ShapeDtypeStruct(coef.shape, jnp.float32),
        ),
        in_specs=[anywhere, anywhere],
        out_specs=(anywhere, anywhere),
        scratch_shapes=[
            pltpu.VMEM(flux.shape, jnp.float32),
            pltpu.VMEM(coef.shape, jnp.float32),
            dma((2, flux.shape[0] + 1)),
        ],
        name="hand_over",
    )(flux, coef)


def solution(mesh):
    in_specs = (P("ax", "az", None), P(None, "ax", "az", None))
    out_specs = (P(None, "ax", "az", None), P("ax", None))
    body = functools.partial(shards, mesh.shape["ax"], mesh.shape["az"])
    return jax.shard_map(body, mesh=mesh, in_specs=in_specs, out_specs=out_specs, check_vma=False)
```
